32 devices in a mesh: terms: 8 (over z, y), sect: 4 (over x, core).
Axes of the slice: x: 2, y: 2, z: 4, core: 2. Of those that a mesh axis runs over, the one named last changes fastest.
Arguments:
- wavefunction: float32 [2, 512, 16, 512], P(None, 'sect'), may hold values from -6 to 6
- left_blocks: float32 [8, 2, 512, 128], P('terms', None, 'sect'), may hold values from -0.125 to 0.125
- right_operators: float32 [8, 2, 512, 512], P('terms'), may hold values from -0.1875 to 0.1875
- site_operators: float32 [8, 2, 16, 16], P('terms'), may hold values from -1 to 1
- term_charge: int32 [8], replicated, may hold values from 0 to 1
- source_terms: int32 [8, 3], replicated, may hold values from 0 to 7, all different within a row
- coupling: float32 [2, 8, 3], replicated, may hold values from -0.01953125 to 0.01953125
- owner: int32 [8], replicated, may hold values from 0 to 7, each once
Outputs:
- sigma: float32 [2, 512, 16, 512], P(None, 'sect', None, 'terms')
- new_right: float32 [8, 2, 512, 128], P('terms', None, 'sect')
The draws below stay inside these ranges and needn't reach their ends.
Inputs may be any that keep to these rules, and one draw needn't show every extreme that they name: `source_terms`: each row names 3 different terms, and every term is named by some row. `owner`: each index along terms owns exactly one new term.
All inputs are finite; a program needn't handle non-finite values.
Results may differ from the reference program's by a relative error of at most 0.0003.
Values sent between devices are 32-bit elements; how exact they have to be, the bound alone decides.
A program may use at most 128 MiB of HBM per device.

```python
import jax
import jax.numpy as jnp
from jax import lax

BOND = 512
PHYS = 16
TOP = 3
K = 8
MB = 128


def plant(drawn, stream_key, low, high):
    longest = drawn.shape.index(max(drawn.shape))
    spots = []
    for shift in (0, 1):
        where = [jax.random.randint(jax.random.fold_in(stream_key, axis), (), 0, length) for axis, length in enumerate(drawn.shape)]
        where[longest] = (where[longest] + shift) % drawn.shape[longest]
        spots.append(tuple(where))
    return drawn.at[spots[0]].set(low).at[spots[1]].set(high)


def levels(rng, shape, split, least, largest):
    gain = 1.0
    for position, blocks in split:
        draws = jax.random.uniform(jax.random.fold_in(jax.random.fold_in(rng, 6), position), (blocks,), jnp.float32, least / len(split), largest / len(split))
        gain = gain * jnp.repeat(jnp.exp(draws), shape[position] // blocks).reshape((-1,) + (1,) * (len(shape) - 1 - position))
    return gain


def distinct(stream_key, rows, amount, top, lift):
    ranking = jax.random.permutation(jax.random.fold_in(stream_key, 1), amount)
    boost = ranking
    for power in range(3):
        boost = boost * boost // amount
    boost = boost * lift // amount
    tickets = jax.random.randint(jax.random.fold_in(stream_key, 2), (rows, amount), 0, 4096) + boost
    fixed_rows = jax.random.permutation(jax.random.fold_in(stream_key, 3), rows)[jnp.arange(amount) % rows]
    tickets = jnp.where(jnp.arange(rows)[:, None] == fixed_rows[None, :], 1 << 14, tickets)
    merit = tickets * amount + jnp.arange(amount)
    return lax.top_k(merit.astype(jnp.int32), top)[1].astype(jnp.int32)


def scatter_about(key, extent, deviation, limit, split=(), held_as=jnp.bfloat16):
    drawn = deviation * jax.random.normal(key, extent, jnp.float32)
    if split:
        drawn = drawn * levels(key, extent, split, -0.22, 0.18)
    return jnp.clip(drawn, -limit, limit).astype(held_as)


def setup_inputs(seed: int = 0) -> dict:
    seeds = jax.random.split(jax.random.key(seed), 9)
    wavefunction = scatter_about(seeds[0], (2, BOND, PHYS, BOND), 1.0, 6.0, ((1, 4),), jnp.float32)
    left_blocks = scatter_about(seeds[1], (K, 2, BOND, MB), (2 * MB * K) ** -0.5, 0.125, ((0, 8), (2, 4)), jnp.float32)
    right_operators = scatter_about(seeds[2], (K, 2, BOND, BOND), (2 * BOND) ** -0.5, 0.1875, ((0, 8),), jnp.float32)
    site_operators = scatter_about(seeds[3], (K, 2, PHYS, PHYS), (2 * PHYS) ** -0.5, 1.0, ((0, 8),), jnp.float32)
    term_charge = plant(jax.random.randint(seeds[4], (K,), 0, 2), jax.random.fold_in(seeds[4], 1), 0, 1).astype(jnp.int32)
    source_terms = distinct(seeds[5], K, K, TOP, 0)
    coupling = scatter_about(seeds[6], (2, K, TOP), (12 * PHYS * BOND) ** -0.5, 0.01953125, (), jnp.float32)
    owner = jax.random.permutation(seeds[7], K).astype(jnp.int32)
    return {"wavefunction": wavefunction, "left_blocks": left_blocks, "right_operators": right_operators, "site_operators": site_operators, "term_charge": term_charge, "source_terms": source_terms, "coupling": coupling, "owner": owner}


def matmul(former, latter):
    return jnp.dot(former, latter, precision=lax.Precision.HIGHEST, preferred_element_type=jnp.float32)


def contract(pattern, former, latter):
    return jnp.einsum(pattern, former, latter, precision=lax.Precision.HIGHEST, preferred_element_type=jnp.float32)


def reference(wavefunction, left_blocks, right_operators, site_operators, term_charge, source_terms, coupling, owner):
    bands = BOND // MB
    flat_re = wavefunction[0].reshape(BOND * PHYS, BOND)
    flat_im = wavefunction[1].reshape(BOND * PHYS, BOND)
    band_re = wavefunction[0].reshape(bands, MB, PHYS * BOND)
    band_im = wavefunction[1].reshape(bands, MB, PHYS * BOND)

    def one_term(running, inputs):
        right_pair, site_pair, left_pair, charge = inputs
        mixed_re = (matmul(flat_re, right_pair[0]) - matmul(flat_im, right_pair[1])).reshape(BOND, PHYS, BOND)
        mixed_im = (matmul(flat_re, right_pair[1]) + matmul(flat_im, right_pair[0])).reshape(BOND, PHYS, BOND)
        acted_re = contract("st,atb->asb", site_pair[0], mixed_re) - contract("st,atb->asb", site_pair[1], mixed_im)
        acted_im = contract("st,atb->asb", site_pair[0], mixed_im) + contract("st,atb->asb", site_pair[1], mixed_re)
        acted_re = acted_re.reshape(bands, MB, PHYS * BOND)
        acted_im = acted_im.reshape(bands, MB, PHYS * BOND)
        left_re = left_pair[0].reshape(bands, MB, MB)
        left_im = left_pair[1].reshape(bands, MB, MB)
        part_re = contract("sae,sex->sax", left_re, acted_re) - contract("sae,sex->sax", left_im, acted_im)
        part_im = contract("sae,sex->sax", left_re, acted_im) + contract("sae,sex->sax", left_im, acted_re)
        contrib = jnp.stack((part_re, part_im))
        zero_band = jnp.zeros((2, 1, MB, PHYS * BOND), jnp.float32)
        lifted = jnp.concatenate((zero_band, contrib[:, :-1]), axis=1)
        running = running + jnp.where(charge == 1, lifted, contrib)
        renorm_re = contract("sax,sex->sae", acted_re, band_re) + contract("sax,sex->sae", acted_im, band_im)
        renorm_im = contract("sax,sex->sae", acted_im, band_re) - contract("sax,sex->sae", acted_re, band_im)
        renorm = jnp.stack((renorm_re, renorm_im)).reshape(2, BOND, MB)
        return running, renorm

    start = jnp.zeros((2, bands, MB, PHYS * BOND), jnp.float32)
    total, renorms = lax.scan(one_term, start, (right_operators, site_operators, left_blocks, term_charge))
    sigma = total.reshape(2, BOND, PHYS, BOND)
    term_ids = jnp.arange(K, dtype=jnp.int32)
    selector = (source_terms[:, :, None] == term_ids[None, None, :]).astype(jnp.float32)
    weight_re = contract("jt,jtk->jk", coupling[0], selector)
    weight_im = contract("jt,jtk->jk", coupling[1], selector)
    new_re = contract("jk,kae->jae", weight_re, renorms[:, 0]) - contract("jk,kae->jae", weight_im, renorms[:, 1])
    new_im = contract("jk,kae->jae", weight_re, renorms[:, 1]) + contract("jk,kae->jae", weight_im, renorms[:, 0])
    new_terms = jnp.stack((new_re, new_im), axis=1)
    placed = (owner[None, :] == term_ids[:, None]).astype(jnp.float32)
    new_right = contract("gj,jcae->gcae", placed, new_terms)
    return sigma, new_right
```

```python
import functools

import jax
import jax.numpy as jnp
from jax import lax
from jax.experimental import pallas as pl
from jax.experimental.pallas import tpu as pltpu
from jax.sharding import PartitionSpec as P

LANES = 128


def split(value):
    high = value.astype(jnp.bfloat16)
    return high, (value - high.astype(jnp.float32)).astype(jnp.bfloat16)


def triple(former, latter, dims=(((1,), (0,)), ((), ()))):
    dot = functools.partial(lax.dot_general, dimension_numbers=dims, preferred_element_type=jnp.float32)
    return dot(former[0], latter[0]) + dot(former[0], latter[1]) + dot(former[1], latter[0])


def act_kernel(wave_ref, ops_ref, coef_ref, y_ref, high, low, mixed):
    groups, _, phys, rows, _ = y_ref.shape

    @pl.when(pl.program_id(0) == 0)
    def _():
        per = ops_ref.shape[0] // groups
        cols = LANES // per
        deep = ops_ref.shape[2]
        for g in range(groups):
            lanes = slice(g * LANES, (g + 1) * LANES)
            for i in range(per):
                part = [
                    jnp.concatenate(
                        [ops_ref[g * per + j, h, :, i * cols : (i + 1) * cols] for j in range(per)], axis=1
                    )
                    for h in range(2)
                ]
                for j, value in enumerate((part[0], part[1], part[0] + part[1])):
                    spot = (j, slice(i * deep, (i + 1) * deep), lanes)
                    high[spot], low[spot] = split(value)

    re, im = wave_ref[0], wave_ref[1]
    t = [triple(split(v), (high[j], low[j])) for j, v in enumerate((re, im, re + im))]
    for j, value in enumerate((t[0] - t[1], t[2] - t[0] - t[1], t[2] - 2.0 * t[1])):
        for g in range(groups):
            mixed[j, g] = value[:, g * LANES : (g + 1) * LANES]

    def block(step, carry):
        g, r = step // (rows // 8), step % (rows // 8)
        base = pl.multiple_of(r * 8 * phys, 8 * phys)
        x = [[mixed[j, g, pl.ds(base + q, 8, stride=phys), :] for q in range(phys)] for j in range(3)]
        out = pl.ds(pl.multiple_of(r * 8, 8), 8)
        for p in range(phys):
            s = []
            for j in range(3):
                total = coef_ref[j, g, p, 0:1, :] * x[j][0]
                for q in range(1, phys):
                    total = total + coef_ref[j, g, p, q : q + 1, :] * x[j][q]
                s.append(total)
            y_ref[g, 0, p, out, :] = s[0] - s[1]
            y_ref[g, 1, p, out, :] = s[2] - s[0] - s[1]
        return carry

    lax.fori_loop(0, groups * (rows // 8), block, 0)


def act(wave, ops, coef, phys):
    _, flat, bond = wave.shape
    rows = flat // phys
    groups = coef.shape[1]
    width = groups * LANES
    step = 32
    return pl.pallas_call(
        act_kernel,
        grid=(rows // step,),
        in_specs=[
            pl.BlockSpec((2, step * phys, bond), lambda i: (0, i, 0)),
            pl.BlockSpec(ops.shape, lambda i: (0, 0, 0, 0)),
            pl.BlockSpec(coef.shape, lambda i: (0, 0, 0, 0, 0)),
        ],
        out_specs=pl.BlockSpec((groups, 2, phys, step, LANES), lambda i: (0, 0, 0, i, 0)),
        out_shape=jax.ShapeDtypeStruct((groups, 2, phys, rows, LANES), jnp.float32),
        scratch_shapes=[
            pltpu.VMEM((3, bond, width), jnp.bfloat16),
            pltpu.VMEM((3, bond, width), jnp.bfloat16),
            pltpu.VMEM((3, groups, step * phys, LANES), jnp.float32),
        ],
        compiler_params=pltpu.CompilerParams(vmem_limit_bytes=58 * 1024 * 1024),
    )(wave, ops, coef)


def close_kernel(charge_ref, weight_ref, y_ref, left_ref, local_ref, stay_ref, up_ref, new_ref, high, low):
    per = left_ref.shape[0]
    terms = new_ref.shape[0]
    phys, rows = y_ref.shape[2], y_ref.shape[3]
    cols = LANES // per
    group = pl.program_id(0)

    @pl.when(group == 0)
    def _():
        high[...], low[...] = split(local_ref[...])
        stay_ref[...] = jnp.zeros_like(stay_ref)
        up_ref[...] = jnp.zeros_like(up_ref)
        new_ref[...] = jnp.zeros_like(new_ref)

    for j in range(per):
        term = group * per + j
        y = jnp.concatenate(
            [
                jnp.concatenate([y_ref[0, h, p, :, j * cols : (j + 1) * cols] for p in range(phys)], axis=1)
                for h in range(2)
            ],
            axis=0,
        )
        y = split(y)
        re, im = left_ref[j, :rows], left_ref[j, rows : 2 * rows]
        left = jnp.concatenate(
            [jnp.concatenate([re, -im], axis=1), jnp.concatenate([im, re], axis=1)], axis=0
        )
        c = triple(split(left), y)
        raised = (charge_ref[term] == 1).astype(jnp.float32)
        up_ref[...] += c * raised
        stay_ref[...] += c * (1.0 - raised)
        gram = triple(y, (high[...], low[...]), (((1,), (1,)), ((), ())))
        q_re = gram[:rows, :rows] + gram[rows:, rows:]
        q_im = gram[rows:, :rows] - gram[:rows, rows:]

        def add(g, carry):
            w_re, w_im = weight_ref[0, g, term], weight_ref[1, g, term]
            new_ref[g, :rows, :] += w_re * q_re - w_im * q_im
            new_ref[g, rows:, :] += w_re * q_im + w_im * q_re
            return carry

        lax.fori_loop(0, terms, add, 0)


def close(charge, weight, y, left, local):
    groups, _, phys, rows, _ = y.shape
    terms, lines, _ = left.shape
    per = terms // groups
    tall, wide = local.shape
    fixed = pl.BlockSpec((tall, wide), lambda i: (0, 0))
    return pl.pallas_call(
        close_kernel,
        grid=(groups,),
        in_specs=[
            pl.BlockSpec(memory_space=pltpu.SMEM),
            pl.BlockSpec(memory_space=pltpu.SMEM),
            pl.BlockSpec((1, 2, phys, rows, LANES), lambda i: (i, 0, 0, 0, 0)),
            pl.BlockSpec((per, lines, rows), lambda i: (i, 0, 0)),
            fixed,
        ],
        out_specs=[pl.BlockSpec(memory_space=pltpu.VMEM)] * 3,
        out_shape=[
            jax.ShapeDtypeStruct((tall, wide), jnp.float32),
            jax.ShapeDtypeStruct((tall, wide), jnp.float32),
            jax.ShapeDtypeStruct((terms, tall, rows), jnp.float32),
        ],
        scratch_shapes=[pltpu.VMEM((tall, wide), jnp.bfloat16)] * 2,
        compiler_params=pltpu.CompilerParams(vmem_limit_bytes=54 * 1024 * 1024),
    )(charge, weight, y, left, local)


def pack_kernel(right_ref, pack_ref):
    terms, _, deep, _ = pack_ref.shape
    cols = right_ref.shape[2] // terms
    per = LANES // cols
    for t in range(terms):
        for h in range(2):
            pieces = [right_ref[h, i * deep : (i + 1) * deep, t * cols : (t + 1) * cols] for i in range(per)]
            pack_ref[t, h] = jnp.concatenate(pieces, axis=1)


def packed(right, terms):
    _, bond, width = right.shape
    deep = bond * width // (terms * LANES)
    vmem = pl.BlockSpec(memory_space=pltpu.VMEM)
    return pl.pallas_call(
        pack_kernel,
        in_specs=[vmem],
        out_specs=vmem,
        out_shape=jax.ShapeDtypeStruct((terms, 2, deep, LANES), jnp.float32),
        compiler_params=pltpu.CompilerParams(vmem_limit_bytes=16 * 1024 * 1024),
    )(right)


def remote(source, target, sends, lands, place):
    return pltpu.make_async_remote_copy(
        src_ref=source,
        dst_ref=target,
        send_sem=sends,
        recv_sem=lands,
        device_id=place,
        device_id_type=pl.DeviceIdType.MESH,
    )


def greet(places):
    barrier = pltpu.get_barrier_semaphore()
    for place in places:
        pl.semaphore_signal(barrier, inc=1, device_id=place, device_id_type=pl.DeviceIdType.MESH)
    pl.semaphore_wait(barrier, len(places))


def gather_kernel(pack_ref, small_ref, ops_ref, smalls_ref, send_a, land_a, send_x, land_x, send_c, land_c, send_f, land_f, send_s, land_s, send_t, land_t, own):
    terms, bands = pack_ref.shape[:2]
    half = terms // 2
    me = lax.axis_index("terms")
    band = lax.axis_index("sect")
    twin = me + 1 - 2 * lax.rem(me, 2)
    near = band + 1 - 2 * lax.rem(band, 2)
    far = lax.rem(band + 2, 4)
    greet([(lax.rem(me + i, terms), band) for i in range(1, terms)] + [(me, near), (me, far)])
    keep = pltpu.make_async_copy(pack_ref.at[me], ops_ref.at[me], own.at[0])
    keep.start()
    keep_small = pltpu.make_async_copy(small_ref, smalls_ref.at[me], own.at[1])
    keep_small.start()
    first = []
    for i in range(1, terms):
        peer = lax.rem(me + i, terms)
        copy = remote(pack_ref.at[peer, band], ops_ref.at[me, band], send_a.at[i - 1], land_a.at[i - 1], (peer, band))
        copy.start()
        first.append(copy)
    tiny = []
    for i in range(half):
        place = (twin if i == 0 else lax.rem(me + 2 * i, terms), band)
        copy = remote(small_ref, smalls_ref.at[me], send_s.at[i], land_s.at[i], place)
        copy.start()
        tiny.append(copy)
    across, beside = [], []
    for i in range(1, terms):
        first[i - 1].wait_recv()
        block = ops_ref.at[lax.rem(me + terms - i, terms), band]
        copy = remote(block, block, send_x.at[i - 1], land_x.at[i - 1], (me, far))
        copy.start()
        across.append(copy)
        copy = remote(block, block, send_c.at[i - 1], land_c.at[i - 1], (me, near))
        copy.start()
        beside.append(copy)
    relay = []
    for i in range(1, half):
        tiny[i].wait_recv()
        block = smalls_ref.at[lax.rem(me + terms - 2 * i, terms)]
        copy = remote(block, block, send_t.at[i - 1], land_t.at[i - 1], (twin, band))
        copy.start()
        relay.append(copy)
    last = []
    for i in range(1, terms):
        across[i - 1].wait_recv()
        block = ops_ref.at[lax.rem(me + terms - i, terms), far]
        copy = remote(block, block, send_f.at[i - 1], land_f.at[i - 1], (me, near))
        copy.start()
        last.append(copy)
    for copy in beside + last + relay + tiny[:1]:
        copy.wait_recv()
    for copy in first + tiny + across + beside + relay + last:
        copy.wait_send()
    keep.wait()
    keep_small.wait()


def gather(pack, small):
    terms = pack.shape[0]
    vmem = pl.BlockSpec(memory_space=pltpu.VMEM)
    pair = [pltpu.SemaphoreType.DMA((terms - 1,))] * 2
    return pl.pallas_call(
        gather_kernel,
        in_specs=[vmem, vmem],
        out_specs=[vmem, vmem],
        out_shape=[
            jax.ShapeDtypeStruct(pack.shape, jnp.float32),
            jax.ShapeDtypeStruct((terms,) + small.shape, jnp.float32),
        ],
        scratch_shapes=pair * 6 + [pltpu.SemaphoreType.DMA((2,))],
        compiler_params=pltpu.CompilerParams(
            collective_id=0, has_side_effects=True, vmem_limit_bytes=24 * 1024 * 1024
        ),
    )(pack, small)


def finish_kernel(stay_ref, up_ref, part_ref, sigma_ref, new_ref, moved, got, held, mine, send_a, land_a, edge):
    terms = part_ref.shape[0]
    me = lax.axis_index("terms")
    band = lax.axis_index("sect")
    bands = lax.axis_size("sect")
    upper = lax.rem(band + 1, bands)
    lower = lax.rem(band + bands - 1, bands)
    greet([(lax.rem(me + i, terms), band) for i in range(1, terms)] + [(me, upper), (me, lower)])
    shift = remote(up_ref, moved, edge.at[0], edge.at[1], (me, upper))
    shift.start()
    copies = []
    for i in range(1, terms):
        peer = lax.rem(me + i, terms)
        copy = remote(part_ref.at[peer], got.at[i - 1], send_a.at[i - 1], land_a.at[i - 1], (peer, band))
        copy.start()
        copies.append(copy)
    keep = pltpu.make_async_copy(stay_ref, held, edge.at[2])
    keep.start()
    keep_part = pltpu.make_async_copy(part_ref.at[me], mine, edge.at[3])
    keep_part.start()
    keep.wait()
    keep_part.wait()
    shift.wait()
    sigma_ref[...] = held[...] + jnp.where(band > 0, moved[...], 0.0)
    total = mine[...]
    for i, copy in enumerate(copies):
        copy.wait()
        total = total + got[i]
    new_ref[...] = total


def finish(stay, up, part):
    terms = part.shape[0]
    vmem = pl.BlockSpec(memory_space=pltpu.VMEM)
    return pl.pallas_call(
        finish_kernel,
        in_specs=[pl.BlockSpec(memory_space=pl.ANY)] * 3,
        out_specs=[vmem] * 2,
        out_shape=[
            jax.ShapeDtypeStruct(stay.shape, jnp.float32),
            jax.ShapeDtypeStruct(part.shape[1:], jnp.float32),
        ],
        scratch_shapes=[
            pltpu.VMEM(stay.shape, jnp.float32),
            pltpu.VMEM((terms - 1,) + part.shape[1:], jnp.float32),
            pltpu.VMEM(stay.shape, jnp.float32),
            pltpu.VMEM(part.shape[1:], jnp.float32),
            pltpu.SemaphoreType.DMA((terms - 1,)),
            pltpu.SemaphoreType.DMA((terms - 1,)),
            pltpu.SemaphoreType.DMA((4,)),
        ],
        compiler_params=pltpu.CompilerParams(
            collective_id=1, has_side_effects=True, vmem_limit_bytes=24 * 1024 * 1024
        ),
    )(stay, up, part)


def fold(value, other):
    dot = functools.partial(jnp.dot, preferred_element_type=jnp.float32)
    return dot(value[0], other[0]) + dot(value[0], other[1]) + dot(value[1], other[0])


def turn(value):
    return pltpu.roll(value, LANES // 2, 1)


def left_lanes(shape):
    return lax.broadcasted_iota(jnp.int32, shape, 1) < LANES // 2


class Ring:
    def __init__(self):
        self.me = lax.axis_index("terms")
        self.band = lax.axis_index("sect")
        self.z, self.y = self.me // 2, lax.rem(self.me, 2)
        flip = 1 - 2 * lax.rem(self.z, 2)
        self.zs = [self.z, self.z + flip, lax.rem(self.z + 2, 4), 3 - self.z]
        self.near = self.band + 1 - 2 * lax.rem(self.band, 2)
        self.far = lax.rem(self.band + 2, 4)

    def z_of(self, pair):
        if isinstance(pair, int):
            return self.zs[pair]
        low, high = lax.rem(pair, 2), pair // 2
        here = self.z + low * (self.zs[1] - self.z)
        there = self.zs[2] + low * (self.zs[3] - self.zs[2])
        return here + high * (there - here)

    def peer(self, slot):
        pair, other = slot // 2, slot % 2 if isinstance(slot, int) else lax.rem(slot, 2)
        y = self.y + other * (1 - 2 * self.y)
        return 2 * self.z_of(pair) + y


def split_rows(wf, wh, wl, start, count):
    rows = pl.ds(start, count)
    re, im = wf[0, rows, :], wf[1, rows, :]
    for j, value in enumerate((re, im, re + im)):
        high, low = split(value)
        wh[j, rows, :] = high
        wl[j, rows, :] = low


def pack_pair(rv, pack, pair, place):
    deep = rv.shape[1] // 2
    lanes = pl.ds(pl.multiple_of(place * LANES, LANES), LANES)
    for h in range(2):
        for part in range(2):
            half = deep // 2
            top = rv[h, part * half : (part + 1) * half, lanes]
            low = rv[h, deep + part * half : deep + (part + 1) * half, lanes]
            left = left_lanes(top.shape)
            pack[pair, 0, 2 * h + part] = jnp.where(left, top, turn(low))
            pack[pair, 1, 2 * h + part] = jnp.where(left, turn(top), low)


def local_weights(wloc, gh, gl, odd, phys):
    rows = wloc.shape[1] // phys

    def one(p, carry):
        re = wloc[0, pl.ds(p, rows, stride=phys), :]
        im = wloc[1, pl.ds(p, rows, stride=phys), :]
        left = left_lanes(re.shape)
        even_value = jnp.where(left, re, turn(im))
        odd_value = jnp.where(left, turn(re), im)
        value = jnp.where(odd == 0, even_value, odd_value).T
        half = LANES // 2
        both = jnp.concatenate([value, jnp.concatenate([-value[half:], value[:half]], axis=0)], axis=1)
        high, low = split(both)
        out = pl.ds(pl.multiple_of(p * LANES, LANES), LANES)
        gh[out, :] = high
        gl[out, :] = low
        return carry

    lax.fori_loop(0, phys, one, 0)


def site_blocks(tiles, dd):
    slots, lines, _ = tiles.shape
    group = 8

    def one(i, carry):
        value = jnp.broadcast_to(tiles[i][:, None, :], (lines, group, LANES))
        column = lax.broadcasted_iota(jnp.int32, value.shape, 2) // (LANES // group)
        row = lax.broadcasted_iota(jnp.int32, value.shape, 1)
        value = jnp.where(column == row, value, 0.0).reshape(lines * group, LANES)
        half = lines * group // 2
        high, low = split(jnp.concatenate([value[:half], value[half:]], axis=1))
        dd[i, :half, :] = high
        dd[i, half:, :] = low
        return carry

    lax.fori_loop(0, slots, one, 0)


def right_planes(ops, rh, rl, batch):
    deep = ops.shape[2]
    for pair in range(2):
        first = batch * 4 + 2 * pair
        lanes = slice(pair * LANES, (pair + 1) * LANES)
        for part in range(2):
            tops, lows = [], []
            for h in range(2):
                a, b = ops[first, 2 * h + part], ops[first + 1, 2 * h + part]
                left = left_lanes(a.shape)
                tops.append(jnp.where(left, a, turn(b)))
                lows.append(jnp.where(left, turn(a), b))
            for offset, (re, im) in ((part * deep, tops), ((2 + part) * deep, lows)):
                for j, value in enumerate((re, im, re + im)):
                    high, low = split(value)
                    rh[j, offset : offset + deep, lanes] = high
                    rl[j, offset : offset + deep, lanes] = low


def act_rows(wh, wl, rh, rl, dd, yh, yl, batch, block, height, phys, rows_all):
    rows = pl.ds(pl.multiple_of(block * height, height), height)
    t = [fold((wh[j, rows, :], wl[j, rows, :]), (rh[j], rl[j])) for j in range(3)]
    re, im = t[0] - t[1], t[2] - t[0] - t[1]
    deep = 8 * phys
    base = block * (height // phys)
    for pair in range(2):
        lanes = slice(pair * LANES, (pair + 1) * LANES)
        a, b = re[:, lanes], im[:, lanes]
        at, bt = turn(a), turn(b)
        left = left_lanes(a.shape)
        for odd in range(2):
            if odd:
                x, ix = jnp.where(left, at, b), jnp.where(left, -bt, a)
            else:
                x, ix = jnp.where(left, a, bt), jnp.where(left, -b, at)
            slot = batch * 4 + 2 * pair + odd
            parts = []
            for v, w in zip(split(x), split(ix)):
                parts.append((v, w))
            for g in range(height // (2 * deep)):
                one, two = g * 2 * deep, (g * 2 + 1) * deep
                sides = []
                for v, w in parts:
                    sides.append(
                        jnp.concatenate(
                            [
                                jnp.concatenate([u[one : one + deep], u[two : two + deep]], axis=1)
                                for u in (v, w)
                            ],
                            axis=0,
                        )
                    )
                dot = functools.partial(jnp.dot, preferred_element_type=jnp.float32)
                wide = dot(dd[slot], sides[0])
                y = wide[:deep] + wide[deep:] + dot(dd[slot, :deep], sides[1])
                y = jnp.concatenate(
                    [y[:, :LANES].reshape(phys, 8, LANES), y[:, LANES:].reshape(phys, 8, LANES)], axis=1
                )
                high, low = split(y)
                out = pl.ds(pl.multiple_of(slot * rows_all + base + g * 16, 16), 16)
                yh[:, out, :] = high
                yl[:, out, :] = low


def overlaps(yh, yl, gh, gl, qs, batch, count):
    phys = yh.shape[0]
    rows = slice(batch * count, (batch + 1) * count)
    wide = [jnp.concatenate([ref[p, rows, :] for p in range(phys)], axis=1) for ref in (yh, yl)]
    qs[rows, :] = fold(wide, (gh[...], gl[...]))


def new_part(weight_ref, qs, nb, slot, ring, rows):
    target = ring.peer(slot)
    slots = nb.shape[0]
    re = jnp.zeros((rows, LANES), jnp.float32)
    im = jnp.zeros((rows, LANES), jnp.float32)
    for i in range(slots):
        term = ring.peer(i)
        w_re, w_im = weight_ref[0, target, term], weight_ref[1, target, term]
        q_re, q_im = qs[i * rows : (i + 1) * rows, :LANES], qs[i * rows : (i + 1) * rows, LANES:]
        re = re + (w_re * q_re - w_im * q_im)
        im = im + (w_re * q_im + w_im * q_re)
    nb[slot, :rows] = re
    nb[slot, rows:] = im


def left_stack(charge_ref, lefts, lh, ll, ring):
    slots, lines, _ = lefts.shape
    for i in range(slots):
        raised = (charge_ref[ring.peer(i)] == 1).astype(jnp.float32)
        value = lefts[i]
        lanes = slice(i * LANES, (i + 1) * LANES)
        for j, part in enumerate((value * (1.0 - raised), value * raised)):
            high, low = split(part)
            lh[j * lines : (j + 1) * lines, lanes] = high
            ll[j * lines : (j + 1) * lines, lanes] = low


def close_pair(lh, ll, yh, yl, stay, up, pair):
    sides = [jnp.concatenate([ref[2 * pair], ref[2 * pair + 1]], axis=1) for ref in (yh, yl)]
    both = fold((lh[...], ll[...]), sides)
    rows = both.shape[0] // 4
    sign = jnp.where(left_lanes((rows, LANES)), -1.0, 1.0)
    for j, target in enumerate((stay, up)):
        for q in range(2):
            lanes = slice(q * LANES, (q + 1) * LANES)
            first = both[2 * j * rows : (2 * j + 1) * rows, lanes]
            second = both[(2 * j + 1) * rows : (2 * j + 2) * rows, lanes]
            target[2 * pair + q] = (first + sign * turn(second)).T


def whole_kernel(
    charge_ref, weight_ref, wave_ref, right_ref, left_ref, tile_ref, sigma_ref, new_ref,
    wf, wloc, wh, wl, rv, pack, ops, tiles, lefts, rh, rl, dd, gh, gl, yh, yl, qs, lh, ll, nb, n1, n2, up, moved,
    local, wave_sem, first_s, first_l, far_s, far_l, near_s, near_l, last_s, last_l,
    tile_s, tile_l, left_s, left_l, twin_s, twin_l, n1_s, n1_l, n2_s, n2_l, up_s, up_l,
):
    ring = Ring()
    me, band = ring.me, ring.band
    slots = ops.shape[0]
    rows = LANES
    phys = yh.shape[0]
    flat = wf.shape[1]
    steps = wave_sem.shape[0]
    chunk = flat // steps

    load_right = pltpu.make_async_copy(right_ref, rv, local.at[0])
    load_right.start()
    lanes = pl.ds(pl.multiple_of(ring.z * LANES, LANES), LANES)
    loads = []
    for i in range(steps):
        part = pl.ds(i * chunk, chunk)
        loads.append(pltpu.make_async_copy(wave_ref.at[:, part, :], wf.at[:, part, :], wave_sem.at[i]))
        loads[-1].start()
    load_local = pltpu.make_async_copy(wave_ref.at[:, :, lanes], wloc, local.at[1])
    load_local.start()
    load_left = pltpu.make_async_copy(left_ref, lefts.at[0], local.at[2])
    load_left.start()
    load_tile = pltpu.make_async_copy(tile_ref, tiles.at[0], local.at[3])
    load_tile.start()

    others = [lax.rem(band + i, 4) for i in range(1, 4)]
    greet([(ring.peer(i), band) for i in range(1, slots)] + [(me, other) for other in others])

    def first(i):
        other = lax.rem(i, 2)
        source = pack.at[i // 2, ring.y + other * (1 - 2 * ring.y), band]
        return remote(source, ops.at[i, band], first_s.at[i - 1], first_l.at[i - 1], (ring.peer(i), band))

    def far(i):
        block = ops.at[i, band]
        return remote(block, block, far_s.at[i - 1], far_l.at[i - 1], (me, ring.far))

    def near(i):
        block = ops.at[i, band]
        return remote(block, block, near_s.at[i - 1], near_l.at[i - 1], (me, ring.near))

    def last(i):
        block = ops.at[i, ring.far]
        return remote(block, block, last_s.at[i - 1], last_l.at[i - 1], (me, ring.near))

    def tile(i):
        return remote(tile_ref, tiles.at[i], tile_s.at[i - 1], tile_l.at[i - 1], (ring.peer(i), band))

    def over(j):
        return remote(left_ref, lefts.at[2 * j], left_s.at[j - 1], left_l.at[j - 1], (2 * ring.z_of(j) + ring.y, band))

    def twin(j):
        source = left_ref if isinstance(j, int) else lefts.at[2 * j]
        return remote(source, lefts.at[2 * j + 1], twin_s.at[j], twin_l.at[j], (ring.peer(1), band))

    load_right.wait()
    keep = pltpu.make_async_copy(pack.at[0, ring.y], ops.at[0], local.at[4])
    for j in range(slots // 2):
        pack_pair(rv, pack, j, ring.zs[j])
        if j == 0:
            keep.start()
            first(1).start()
        else:
            first(2 * j).start()
            first(2 * j + 1).start()
    for i in range(1, slots):
        tile(i).start()

    def forward(i):
        first(i).wait_recv()
        far(i).start()
        near(i).start()

    for i in range(steps):
        loads[i].wait()
        split_rows(wf, wh, wl, i * chunk, chunk)
        if 1 <= i < 4:
            forward(i)
    load_local.wait()
    for i in range(1, 4):
        far(i).wait_recv()
        last(i).start()
    local_weights(wloc, gh, gl, ring.y, phys)
    load_tile.wait()
    for i in range(1, slots):
        tile(i).wait_recv()
    site_blocks(tiles, dd)
    keep.wait()
    for i in range(1, 4):
        near(i).wait_recv()
        last(i).wait_recv()
    right_planes(ops, rh, rl, 0)

    height = flat // 4

    def early(block, carry):
        forward(block + 4)
        act_rows(wh, wl, rh, rl, dd, yh, yl, 0, block, height, phys, rows)
        return carry

    lax.fori_loop(0, 4, early, 0)
    for i in range(4, 8):
        far(i).wait_recv()
        last(i).start()
    for j in range(1, 4):
        over(j).start()
    twin(0).start()
    for i in range(4, 8):
        near(i).wait_recv()
        last(i).wait_recv()
    right_planes(ops, rh, rl, 1)

    def late(block, carry):
        @pl.when(block > 0)
        def _():
            over(block).wait_recv()
            twin(block).start()

        act_rows(wh, wl, rh, rl, dd, yh, yl, 1, block, height, phys, rows)
        return carry

    lax.fori_loop(0, 4, late, 0)
    half = slots // 2 * rows
    overlaps(yh, yl, gh, gl, qs, 0, half)
    overlaps(yh, yl, gh, gl, qs, 1, half)

    order = (2, 3, 1, 0)

    def fold_one(j):
        return remote(nb.at[2 * j + 1], n1.at[j], n1_s.at[j], n1_l.at[j], (ring.peer(1), band))

    def fold_two(j):
        return remote(nb.at[2 * j], n2.at[j - 1], n2_s.at[j - 1], n2_l.at[j - 1], (ring.peer(2 * j), band))

    for j in order:
        new_part(weight_ref, qs, nb, 2 * j + 1, ring, rows)
        fold_one(j).start()
    for j in order:
        new_part(weight_ref, qs, nb, 2 * j, ring, rows)
    load_left.wait()
    for j in range(4):
        twin(j if j == 0 else jnp.int32(j)).wait_recv()
    left_stack(charge_ref, lefts, lh, ll, ring)

    above = lax.rem(band + 1, 4)

    def lift(pair):
        part = pl.ds(2 * pair, 2)
        return remote(up.at[part], moved.at[part], up_s.at[pair], up_l.at[pair], (me, above))

    def close_step(pair, carry):
        close_pair(lh, ll, yh, yl, sigma_ref, up, pair)

        @pl.when(band < 3)
        def _():
            lift(pair).start()

        for at, j in zip((1, 3, 5, 7), order):
            @pl.when(pair == at)
            def _():
                fold_one(j).wait_recv()
                nb[2 * j] += n1[j]
                if j:
                    fold_two(j).start()

        return carry

    lax.fori_loop(0, phys // 2, close_step, 0)

    @pl.when(band > 0)
    def _():
        def gain(pair, carry):
            lift(pair).wait_recv()
            part = pl.ds(2 * pair, 2)
            sigma_ref[part] += moved[part]
            return carry

        lax.fori_loop(0, phys // 2, gain, 0)

    total = nb[0]
    for j in order[:3]:
        fold_two(j).wait_recv()
        total = total + n2[j - 1]
    new_ref[...] = total

    for i in range(1, slots):
        for copy in (first(i), far(i), near(i), last(i), tile(i)):
            copy.wait_send()
    for j in range(4):
        fold_one(j).wait_send()
        twin(j).wait_send()
        if j:
            over(j).wait_send()
            fold_two(j).wait_send()

    @pl.when(band < 3)
    def _():
        for pair in range(phys // 2):
            lift(pair).wait_send()


def whole(charge, weight, wave, right, left, tile):
    _, flat, bond = wave.shape
    terms = weight.shape[1]
    phys = tile.shape[0] // 2
    rows = flat // phys
    lines = terms * rows
    f32, bf16 = jnp.float32, jnp.bfloat16
    hbm = pl.BlockSpec(memory_space=pl.ANY)
    smem = pl.BlockSpec(memory_space=pltpu.SMEM)
    vmem = pl.BlockSpec(memory_space=pltpu.VMEM)
    dma = lambda n: pltpu.SemaphoreType.DMA((n,))
    return pl.pallas_call(
        whole_kernel,
        in_specs=[smem, smem, hbm, hbm, hbm, hbm],
        out_specs=[vmem, vmem],
        out_shape=[
            jax.ShapeDtypeStruct((phys, LANES, rows), f32),
            jax.ShapeDtypeStruct((2 * rows, rows), f32),
        ],
        scratch_shapes=[
            pltpu.VMEM(wave.shape, f32),
            pltpu.VMEM((2, flat, LANES), f32),
            pltpu.VMEM((3, flat, bond), bf16),
            pltpu.VMEM((3, flat, bond), bf16),
            pltpu.VMEM(right.shape, f32),
            pltpu.VMEM((terms // 2, 2, 4, bond // 4, LANES), f32),
            pltpu.VMEM((terms, 4, bond // 4, LANES), f32),
            pltpu.VMEM((terms,) + tile.shape, f32),
            pltpu.VMEM((terms,) + left.shape, f32),
            pltpu.VMEM((3, bond, 2 * LANES), bf16),
            pltpu.VMEM((3, bond, 2 * LANES), bf16),
            pltpu.VMEM((terms, 16 * phys, 16 * phys), bf16),
            pltpu.VMEM((flat, 2 * rows), bf16),
            pltpu.VMEM((flat, 2 * rows), bf16),
            pltpu.VMEM((phys, lines, LANES), bf16),
            pltpu.VMEM((phys, lines, LANES), bf16),
            pltpu.VMEM((lines, 2 * LANES), f32),
            pltpu.VMEM((4 * rows, lines), bf16),
            pltpu.VMEM((4 * rows, lines), bf16),
            pltpu.VMEM((terms, 2 * rows, rows), f32),
            pltpu.VMEM((terms // 2, 2 * rows, rows), f32),
            pltpu.VMEM((terms // 2 - 1, 2 * rows, rows), f32),
            pltpu.VMEM((phys, LANES, rows), f32),
            pltpu.VMEM((phys, LANES, rows), f32),
            dma(5),
            dma(4),
        ]
        + [dma(terms - 1)] * 10
        + [dma(terms // 2 - 1)] * 2
        + [dma(terms // 2)] * 4
        + [dma(terms // 2 - 1)] * 2
        + [dma(phys // 2)] * 2,
        compiler_params=pltpu.CompilerParams(
            collective_id=2, has_side_effects=True, vmem_limit_bytes=60 * 1024 * 1024
        ),
    )(charge, weight, wave, right, left, tile)


def new_weights(source, coupling, owner, terms):
    term_ids = jnp.arange(terms, dtype=jnp.int32)
    hit = (source[:, :, None] == term_ids).astype(jnp.float32)
    place = (owner[None, :] == term_ids[:, None]).astype(jnp.float32)
    weight = jnp.sum(coupling[:, :, :, None] * hit, axis=2)
    return jnp.sum(place[None, :, :, None] * weight[:, None], axis=2)


def block(wave, left, right, site, charge, source, coupling, owner):
    _, rows, phys, bond = wave.shape
    terms = lax.axis_size("terms")
    cols = bond // terms
    weight = new_weights(source, coupling, owner, terms)
    tile = jnp.tile(site[0].reshape(2 * phys, phys), (1, LANES // phys))
    sigma, new = whole(
        charge, weight, wave.reshape(2, rows * phys, bond), right[0], left[0].reshape(2 * rows, rows), tile
    )
    sigma = sigma.reshape(phys, 2, cols, rows).transpose(1, 3, 0, 2)
    return sigma, new.reshape(1, 2, rows, rows)


def body(wave, left, right, site, charge, source, coupling, owner):
    _, rows, phys, bond = wave.shape
    terms = lax.axis_size("terms")
    bands = lax.axis_size("sect")
    me = lax.axis_index("terms")
    cols = bond // terms
    per = LANES // cols
    pack = packed(right[0], terms).reshape(terms, bands, -1, LANES)
    lines = site.size // LANES
    room = -lines % 8
    small = jnp.concatenate(
        (left[0].reshape(2 * rows, rows), site.reshape(lines, LANES), jnp.zeros((room, LANES), jnp.float32))
    )
    ops, smalls = gather(pack, small)
    sites = smalls[:, 2 * rows : 2 * rows + lines].reshape(terms // per, per, 2, phys, phys)
    weights = jnp.stack((sites[:, :, 0], sites[:, :, 1], sites[:, :, 0] + sites[:, :, 1]))
    slot = jnp.arange(LANES, dtype=jnp.int32) // cols
    coef = sum(jnp.where(slot == j, weights[:, :, j, :, :, None], 0.0) for j in range(per))
    y = act(wave.reshape(2, rows * phys, bond), ops.reshape(terms, 2, bond // per, LANES), coef, phys)
    local = lax.dynamic_slice_in_dim(wave, me * cols, cols, axis=3).reshape(2 * rows, phys * cols)
    term_ids = jnp.arange(terms, dtype=jnp.int32)
    hit = (source[:, :, None] == term_ids).astype(jnp.float32)
    place = (owner[None, :] == term_ids[:, None]).astype(jnp.float32)
    weight = jnp.sum(coupling[:, :, :, None] * hit, axis=2)
    weight = jnp.sum(place[None, :, :, None] * weight[:, None], axis=2)
    stay, up, part = close(charge, weight, y, smalls, local)
    sigma, new = finish(stay, up, part)
    return sigma.reshape(2, rows, phys, cols), new.reshape(1, 2, rows, rows)


def solution(mesh):
    placed = (
        P(None, "sect", None, None),
        P("terms", None, "sect", None),
        P("terms", None, None, None),
        P("terms", None, None, None),
        P(),
        P(),
        P(),
        P(),
    )
    fits = mesh.shape["terms"] == 8 and mesh.shape["sect"] == 4
    return jax.shard_map(
        block if fits else body,
        mesh=mesh,
        in_specs=placed,
        out_specs=(P(None, "sect", None, "terms"), P("terms", None, "sect", None)),
        check_vma=False,
    )
```

```python
import functools

import jax
import jax.numpy as jnp
from jax import lax
from jax.experimental import pallas as pl
from jax.experimental.pallas import tpu as pltpu
from jax.sharding import PartitionSpec as P

LANES = 128


def split(value):
    high = value.astype(jnp.bfloat16)
    return high, (value - high.astype(jnp.float32)).astype(jnp.bfloat16)


def triple(former, latter, dims=(((1,), (0,)), ((), ()))):
    dot = functools.partial(lax.dot_general, dimension_numbers=dims, preferred_element_type=jnp.float32)
    return dot(former[0], latter[0]) + dot(former[0], latter[1]) + dot(former[1], latter[0])


def act_kernel(wave_ref, ops_ref, coef_ref, y_ref, high, low, mixed):
    groups, _, phys, rows, _ = y_ref.shape

    @pl.when(pl.program_id(0) == 0)
    def _():
        per = ops_ref.shape[0] // groups
        cols = LANES // per
        deep = ops_ref.shape[2]
        for g in range(groups):
            lanes = slice(g * LANES, (g + 1) * LANES)
            for i in range(per):
                part = [
                    jnp.concatenate(
                        [ops_ref[g * per + j, h, :, i * cols : (i + 1) * cols] for j in range(per)], axis=1
                    )
                    for h in range(2)
                ]
                for j, value in enumerate((part[0], part[1], part[0] + part[1])):
                    spot = (j, slice(i * deep, (i + 1) * deep), lanes)
                    high[spot], low[spot] = split(value)

    re, im = wave_ref[0], wave_ref[1]
    t = [triple(split(v), (high[j], low[j])) for j, v in enumerate((re, im, re + im))]
    for j, value in enumerate((t[0] - t[1], t[2] - t[0] - t[1], t[2] - 2.0 * t[1])):
        for g in range(groups):
            mixed[j, g] = value[:, g * LANES : (g + 1) * LANES]

    def block(step, carry):
        g, r = step // (rows // 8), step % (rows // 8)
        base = pl.multiple_of(r * 8 * phys, 8 * phys)
        x = [[mixed[j, g, pl.ds(base + q, 8, stride=phys), :] for q in range(phys)] for j in range(3)]
        out = pl.ds(pl.multiple_of(r * 8, 8), 8)
        for p in range(phys):
            s = []
            for j in range(3):
                total = coef_ref[j, g, p, 0:1, :] * x[j][0]
                for q in range(1, phys):
                    total = total + coef_ref[j, g, p, q : q + 1, :] * x[j][q]
                s.append(total)
            y_ref[g, 0, p, out, :] = s[0] - s[1]
            y_ref[g, 1, p, out, :] = s[2] - s[0] - s[1]
        return carry

    lax.fori_loop(0, groups * (rows // 8), block, 0)


def act(wave, ops, coef, phys):
    _, flat, bond = wave.shape
    rows = flat // phys
    groups = coef.shape[1]
    width = groups * LANES
    step = 32
    return pl.pallas_call(
        act_kernel,
        grid=(rows // step,),
        in_specs=[
            pl.BlockSpec((2, step * phys, bond), lambda i: (0, i, 0)),
            pl.BlockSpec(ops.shape, lambda i: (0, 0, 0, 0)),
            pl.BlockSpec(coef.shape, lambda i: (0, 0, 0, 0, 0)),
        ],
        out_specs=pl.BlockSpec((groups, 2, phys, step, LANES), lambda i: (0, 0, 0, i, 0)),
        out_shape=jax.ShapeDtypeStruct((groups, 2, phys, rows, LANES), jnp.float32),
        scratch_shapes=[
            pltpu.VMEM((3, bond, width), jnp.bfloat16),
            pltpu.VMEM((3, bond, width), jnp.bfloat16),
            pltpu.VMEM((3, groups, step * phys, LANES), jnp.float32),
        ],
        compiler_params=pltpu.CompilerParams(vmem_limit_bytes=58 * 1024 * 1024),
    )(wave, ops, coef)


def close_kernel(charge_ref, weight_ref, y_ref, left_ref, local_ref, stay_ref, up_ref, new_ref, high, low):
    per = left_ref.shape[0]
    terms = new_ref.shape[0]
    phys, rows = y_ref.shape[2], y_ref.shape[3]
    cols = LANES // per
    group = pl.program_id(0)

    @pl.when(group == 0)
    def _():
        high[...], low[...] = split(local_ref[...])
        stay_ref[...] = jnp.zeros_like(stay_ref)
        up_ref[...] = jnp.zeros_like(up_ref)
        new_ref[...] = jnp.zeros_like(new_ref)

    for j in range(per):
        term = group * per + j
        y = jnp.concatenate(
            [
                jnp.concatenate([y_ref[0, h, p, :, j * cols : (j + 1) * cols] for p in range(phys)], axis=1)
                for h in range(2)
            ],
            axis=0,
        )
        y = split(y)
        re, im = left_ref[j, :rows], left_ref[j, rows : 2 * rows]
        left = jnp.concatenate(
            [jnp.concatenate([re, -im], axis=1), jnp.concatenate([im, re], axis=1)], axis=0
        )
        c = triple(split(left), y)
        raised = (charge_ref[term] == 1).astype(jnp.float32)
        up_ref[...] += c * raised
        stay_ref[...] += c * (1.0 - raised)
        gram = triple(y, (high[...], low[...]), (((1,), (1,)), ((), ())))
        q_re = gram[:rows, :rows] + gram[rows:, rows:]
        q_im = gram[rows:, :rows] - gram[:rows, rows:]

        def add(g, carry):
            w_re, w_im = weight_ref[0, g, term], weight_ref[1, g, term]
            new_ref[g, :rows, :] += w_re * q_re - w_im * q_im
            new_ref[g, rows:, :] += w_re * q_im + w_im * q_re
            return carry

        lax.fori_loop(0, terms, add, 0)


def close(charge, weight, y, left, local):
    groups, _, phys, rows, _ = y.shape
    terms, lines, _ = left.shape
    per = terms // groups
    tall, wide = local.shape
    fixed = pl.BlockSpec((tall, wide), lambda i: (0, 0))
    return pl.pallas_call(
        close_kernel,
        grid=(groups,),
        in_specs=[
            pl.BlockSpec(memory_space=pltpu.SMEM),
            pl.BlockSpec(memory_space=pltpu.SMEM),
            pl.BlockSpec((1, 2, phys, rows, LANES), lambda i: (i, 0, 0, 0, 0)),
            pl.BlockSpec((per, lines, rows), lambda i: (i, 0, 0)),
            fixed,
        ],
        out_specs=[pl.BlockSpec(memory_space=pltpu.VMEM)] * 3,
        out_shape=[
            jax.ShapeDtypeStruct((tall, wide), jnp.float32),
            jax.ShapeDtypeStruct((tall, wide), jnp.float32),
            jax.ShapeDtypeStruct((terms, tall, rows), jnp.float32),
        ],
        scratch_shapes=[pltpu.VMEM((tall, wide), jnp.bfloat16)] * 2,
        compiler_params=pltpu.CompilerParams(vmem_limit_bytes=54 * 1024 * 1024),
    )(charge, weight, y, left, local)


def pack_kernel(right_ref, pack_ref):
    terms, _, deep, _ = pack_ref.shape
    cols = right_ref.shape[2] // terms
    per = LANES // cols
    for t in range(terms):
        for h in range(2):
            pieces = [right_ref[h, i * deep : (i + 1) * deep, t * cols : (t + 1) * cols] for i in range(per)]
            pack_ref[t, h] = jnp.concatenate(pieces, axis=1)


def packed(right, terms):
    _, bond, width = right.shape
    deep = bond * width // (terms * LANES)
    vmem = pl.BlockSpec(memory_space=pltpu.VMEM)
    return pl.pallas_call(
        pack_kernel,
        in_specs=[vmem],
        out_specs=vmem,
        out_shape=jax.ShapeDtypeStruct((terms, 2, deep, LANES), jnp.float32),
        compiler_params=pltpu.CompilerParams(vmem_limit_bytes=16 * 1024 * 1024),
    )(right)


def remote(source, target, sends, lands, place):
    return pltpu.make_async_remote_copy(
        src_ref=source,
        dst_ref=target,
        send_sem=sends,
        recv_sem=lands,
        device_id=place,
        device_id_type=pl.DeviceIdType.MESH,
    )


def greet(places):
    barrier = pltpu.get_barrier_semaphore()
    for place in places:
        pl.semaphore_signal(barrier, inc=1, device_id=place, device_id_type=pl.DeviceIdType.MESH)
    pl.semaphore_wait(barrier, len(places))


def gather_kernel(pack_ref, small_ref, ops_ref, smalls_ref, send_a, land_a, send_x, land_x, send_c, land_c, send_f, land_f, send_s, land_s, send_t, land_t, own):
    terms, bands = pack_ref.shape[:2]
    half = terms // 2
    me = lax.axis_index("terms")
    band = lax.axis_index("sect")
    twin = me + 1 - 2 * lax.rem(me, 2)
    near = band + 1 - 2 * lax.rem(band, 2)
    far = lax.rem(band + 2, 4)
    greet([(lax.rem(me + i, terms), band) for i in range(1, terms)] + [(me, near), (me, far)])
    keep = pltpu.make_async_copy(pack_ref.at[me], ops_ref.at[me], own.at[0])
    keep.start()
    keep_small = pltpu.make_async_copy(small_ref, smalls_ref.at[me], own.at[1])
    keep_small.start()
    first = []
    for i in range(1, terms):
        peer = lax.rem(me + i, terms)
        copy = remote(pack_ref.at[peer, band], ops_ref.at[me, band], send_a.at[i - 1], land_a.at[i - 1], (peer, band))
        copy.start()
        first.append(copy)
    tiny = []
    for i in range(half):
        place = (twin if i == 0 else lax.rem(me + 2 * i, terms), band)
        copy = remote(small_ref, smalls_ref.at[me], send_s.at[i], land_s.at[i], place)
        copy.start()
        tiny.append(copy)
    across, beside = [], []
    for i in range(1, terms):
        first[i - 1].wait_recv()
        block = ops_ref.at[lax.rem(me + terms - i, terms), band]
        copy = remote(block, block, send_x.at[i - 1], land_x.at[i - 1], (me, far))
        copy.start()
        across.append(copy)
        copy = remote(block, block, send_c.at[i - 1], land_c.at[i - 1], (me, near))
        copy.start()
        beside.append(copy)
    relay = []
    for i in range(1, half):
        tiny[i].wait_recv()
        block = smalls_ref.at[lax.rem(me + terms - 2 * i, terms)]
        copy = remote(block, block, send_t.at[i - 1], land_t.at[i - 1], (twin, band))
        copy.start()
        relay.append(copy)
    last = []
    for i in range(1, terms):
        across[i - 1].wait_recv()
        block = ops_ref.at[lax.rem(me + terms - i, terms), far]
        copy = remote(block, block, send_f.at[i - 1], land_f.at[i - 1], (me, near))
        copy.start()
        last.append(copy)
    for copy in beside + last + relay + tiny[:1]:
        copy.wait_recv()
    for copy in first + tiny + across + beside + relay + last:
        copy.wait_send()
    keep.wait()
    keep_small.wait()


def gather(pack, small):
    terms = pack.shape[0]
    vmem = pl.BlockSpec(memory_space=pltpu.VMEM)
    pair = [pltpu.SemaphoreType.DMA((terms - 1,))] * 2
    return pl.pallas_call(
        gather_kernel,
        in_specs=[vmem, vmem],
        out_specs=[vmem, vmem],
        out_shape=[
            jax.ShapeDtypeStruct(pack.shape, jnp.float32),
            jax.ShapeDtypeStruct((terms,) + small.shape, jnp.float32),
        ],
        scratch_shapes=pair * 6 + [pltpu.SemaphoreType.DMA((2,))],
        compiler_params=pltpu.CompilerParams(
            collective_id=0, has_side_effects=True, vmem_limit_bytes=24 * 1024 * 1024
        ),
    )(pack, small)


def finish_kernel(stay_ref, up_ref, part_ref, sigma_ref, new_ref, moved, got, held, mine, send_a, land_a, edge):
    terms = part_ref.shape[0]
    me = lax.axis_index("terms")
    band = lax.axis_index("sect")
    bands = lax.axis_size("sect")
    upper = lax.rem(band + 1, bands)
    lower = lax.rem(band + bands - 1, bands)
    greet([(lax.rem(me + i, terms), band) for i in range(1, terms)] + [(me, upper), (me, lower)])
    shift = remote(up_ref, moved, edge.at[0], edge.at[1], (me, upper))
    shift.start()
    copies = []
    for i in range(1, terms):
        peer = lax.rem(me + i, terms)
        copy = remote(part_ref.at[peer], got.at[i - 1], send_a.at[i - 1], land_a.at[i - 1], (peer, band))
        copy.start()
        copies.append(copy)
    keep = pltpu.make_async_copy(stay_ref, held, edge.at[2])
    keep.start()
    keep_part = pltpu.make_async_copy(part_ref.at[me], mine, edge.at[3])
    keep_part.start()
    keep.wait()
    keep_part.wait()
    shift.wait()
    sigma_ref[...] = held[...] + jnp.where(band > 0, moved[...], 0.0)
    total = mine[...]
    for i, copy in enumerate(copies):
        copy.wait()
        total = total + got[i]
    new_ref[...] = total


def finish(stay, up, part):
    terms = part.shape[0]
    vmem = pl.BlockSpec(memory_space=pltpu.VMEM)
    return pl.pallas_call(
        finish_kernel,
        in_specs=[pl.BlockSpec(memory_space=pl.ANY)] * 3,
        out_specs=[vmem] * 2,
        out_shape=[
            jax.ShapeDtypeStruct(stay.shape, jnp.float32),
            jax.ShapeDtypeStruct(part.shape[1:], jnp.float32),
        ],
        scratch_shapes=[
            pltpu.VMEM(stay.shape, jnp.float32),
            pltpu.VMEM((terms - 1,) + part.shape[1:], jnp.float32),
            pltpu.VMEM(stay.shape, jnp.float32),
            pltpu.VMEM(part.shape[1:], jnp.float32),
            pltpu.SemaphoreType.DMA((terms - 1,)),
            pltpu.SemaphoreType.DMA((terms - 1,)),
            pltpu.SemaphoreType.DMA((4,)),
        ],
        compiler_params=pltpu.CompilerParams(
            collective_id=1, has_side_effects=True, vmem_limit_bytes=24 * 1024 * 1024
        ),
    )(stay, up, part)


def fold(value, other):
    dot = functools.partial(jnp.dot, preferred_element_type=jnp.float32)
    return dot(value[0], other[0]) + dot(value[0], other[1]) + dot(value[1], other[0])


def turn(value):
    return pltpu.roll(value, LANES // 2, 1)


def left_lanes(shape):
    return lax.broadcasted_iota(jnp.int32, shape, 1) < LANES // 2


class Ring:
    def __init__(self):
        self.me = lax.axis_index("terms")
        self.band = lax.axis_index("sect")
        self.z, self.y = self.me // 2, lax.rem(self.me, 2)
        flip = 1 - 2 * lax.rem(self.z, 2)
        self.zs = [self.z, self.z + flip, lax.rem(self.z + 2, 4), 3 - self.z]
        self.near = self.band + 1 - 2 * lax.rem(self.band, 2)
        self.far = lax.rem(self.band + 2, 4)

    def z_of(self, pair):
        if isinstance(pair, int):
            return self.zs[pair]
        low, high = lax.rem(pair, 2), pair // 2
        here = self.z + low * (self.zs[1] - self.z)
        there = self.zs[2] + low * (self.zs[3] - self.zs[2])
        return here + high * (there - here)

    def peer(self, slot):
        pair, other = slot // 2, slot % 2 if isinstance(slot, int) else lax.rem(slot, 2)
        y = self.y + other * (1 - 2 * self.y)
        return 2 * self.z_of(pair) + y


def split_rows(wf, wh, wl, slot, start):
    re, im = wf[slot, 0], wf[slot, 1]
    rows = pl.ds(start, re.shape[0])
    for j, value in enumerate((re, im, re + im)):
        high, low = split(value)
        wh[j, rows, :] = high
        wl[j, rows, :] = low


def pack_pair(rv, pack, pair, place):
    deep = rv.shape[1] // 2
    lanes = pl.ds(pl.multiple_of(place * LANES, LANES), LANES)
    for h in range(2):
        for part in range(2):
            half = deep // 2
            top = rv[h, part * half : (part + 1) * half, lanes]
            low = rv[h, deep + part * half : deep + (part + 1) * half, lanes]
            left = left_lanes(top.shape)
            pack[pair, 0, 2 * h + part] = jnp.where(left, top, turn(low))
            pack[pair, 1, 2 * h + part] = jnp.where(left, turn(top), low)


def local_weights(wloc, gh, gl, odd, phys, start, end):
    rows = wloc.shape[1] // phys

    def one(p, carry):
        re = wloc[0, pl.ds(p, rows, stride=phys), :]
        im = wloc[1, pl.ds(p, rows, stride=phys), :]
        left = left_lanes(re.shape)
        even_value = jnp.where(left, re, turn(im))
        odd_value = jnp.where(left, turn(re), im)
        value = jnp.where(odd == 0, even_value, odd_value).T
        half = LANES // 2
        both = jnp.concatenate([value, jnp.concatenate([-value[half:], value[:half]], axis=0)], axis=1)
        high, low = split(both)
        out = pl.ds(pl.multiple_of(p * LANES, LANES), LANES)
        gh[out, :] = high
        gl[out, :] = low
        return carry

    lax.fori_loop(start, end, one, 0)


def site_blocks(tiles, dd):
    slots, lines, _ = tiles.shape
    group = 8

    def one(i, carry):
        value = jnp.broadcast_to(tiles[i][:, None, :], (lines, group, LANES))
        column = lax.broadcasted_iota(jnp.int32, value.shape, 2) // (LANES // group)
        row = lax.broadcasted_iota(jnp.int32, value.shape, 1)
        value = jnp.where(column == row, value, 0.0).reshape(lines * group, LANES)
        half = lines * group // 2
        high, low = split(jnp.concatenate([value[:half], value[half:]], axis=1))
        dd[i, :half, :] = high
        dd[i, half:, :] = low
        return carry

    lax.fori_loop(0, slots, one, 0)


def right_planes(ops, rh, rl, batch):
    deep = ops.shape[2]
    for pair in range(2):
        first = batch * 4 + 2 * pair
        lanes = slice(pair * LANES, (pair + 1) * LANES)
        for part in range(2):
            tops, lows = [], []
            for h in range(2):
                a, b = ops[first, 2 * h + part], ops[first + 1, 2 * h + part]
                left = left_lanes(a.shape)
                tops.append(jnp.where(left, a, turn(b)))
                lows.append(jnp.where(left, turn(a), b))
            for offset, (re, im) in ((part * deep, tops), ((2 + part) * deep, lows)):
                for j, value in enumerate((re, im, re + im)):
                    high, low = split(value)
                    rh[batch, j, offset : offset + deep, lanes] = high
                    rl[batch, j, offset : offset + deep, lanes] = low


def act_rows(wh, wl, rh, rl, xs, step, height):
    batch = step // 4
    rows = pl.ds(pl.multiple_of(lax.rem(step, 4) * height, height), height)
    t = [fold((wh[j, rows, :], wl[j, rows, :]), (rh[batch, j], rl[batch, j])) for j in range(3)]
    re, im = t[0] - t[1], t[2] - t[0] - t[1]
    for pair in range(2):
        lanes = slice(pair * LANES, (pair + 1) * LANES)
        a, b = re[:, lanes], im[:, lanes]
        at, bt = turn(a), turn(b)
        left = left_lanes(a.shape)
        xs[2 * pair, 0, 0], xs[2 * pair, 0, 1] = split(jnp.where(left, a, bt))
        xs[2 * pair, 1, 0], xs[2 * pair, 1, 1] = split(jnp.where(left, -b, at))
        xs[2 * pair + 1, 0, 0], xs[2 * pair + 1, 0, 1] = split(jnp.where(left, at, b))
        xs[2 * pair + 1, 1, 0], xs[2 * pair + 1, 1, 1] = split(jnp.where(left, -bt, a))


def site_rows(dd, xs, yh, yl, step, phys, rows):
    dot = functools.partial(jnp.dot, preferred_element_type=jnp.float32)
    height = xs.shape[3]
    deep = 8 * phys
    base = lax.rem(step, 4) * (height // phys)
    for i in range(4):
        slot = (step // 4) * 4 + i
        for g in range(height // (2 * deep)):
            one, two = g * 2 * deep, (g * 2 + 1) * deep
            sides = [
                jnp.concatenate(
                    [
                        jnp.concatenate([xs[i, j, h, one : one + deep], xs[i, j, h, two : two + deep]], axis=1)
                        for j in range(2)
                    ],
                    axis=0,
                )
                for h in range(2)
            ]
            wide = dot(dd[slot], sides[0])
            y = wide[:deep] + wide[deep:] + dot(dd[slot, :deep], sides[1])
            y = jnp.concatenate(
                [y[:, :LANES].reshape(phys, 8, LANES), y[:, LANES:].reshape(phys, 8, LANES)], axis=1
            )
            high, low = split(y)
            out = pl.ds(pl.multiple_of(slot * rows + base + g * 16, 16), 16)
            yh[:, out, :] = high
            yl[:, out, :] = low


def overlaps(yh, yl, gh, gl, qs, pieces):
    phys = yh.shape[0]
    wide = [
        jnp.concatenate(
            [jnp.concatenate([ref[p, a : a + n, :] for a, n in pieces], axis=0) for p in range(phys)], axis=1
        )
        for ref in (yh, yl)
    ]
    value = fold(wide, (gh[...], gl[...]))
    done = 0
    for a, n in pieces:
        qs[a : a + n, :] = value[done : done + n]
        done += n


def new_part(source_ref, coupling_ref, owner_ref, qs, nb, slot, half, ring, rows):
    target = ring.peer(slot)
    slots, top = owner_ref.shape[0], source_ref.shape[0]
    fresh = jnp.int32(0)
    for j in range(1, slots):
        fresh = jnp.where(owner_ref[j] == target, j, fresh)
    sources = [source_ref[t, fresh] for t in range(top)]
    factors = [(coupling_ref[t, 0, fresh], coupling_ref[t, 1, fresh]) for t in range(top)]
    count = rows // 2
    re = jnp.zeros((count, LANES), jnp.float32)
    im = jnp.zeros((count, LANES), jnp.float32)
    for i in range(slots):
        term = ring.peer(i)
        w_re, w_im = jnp.float32(0.0), jnp.float32(0.0)
        for term_t, (f_re, f_im) in zip(sources, factors):
            w_re = w_re + jnp.where(term_t == term, f_re, 0.0)
            w_im = w_im + jnp.where(term_t == term, f_im, 0.0)
        part = slice(i * rows + half * count, i * rows + (half + 1) * count)
        q_re, q_im = qs[part, :LANES], qs[part, LANES:]
        re = re + (w_re * q_re - w_im * q_im)
        im = im + (w_re * q_im + w_im * q_re)
    nb[slot, half, 0] = re
    nb[slot, half, 1] = im


def left_stack(charge_ref, lefts, lh, ll, ring):
    slots, lines, _ = lefts.shape
    for i in range(slots):
        raised = (charge_ref[ring.peer(i)] == 1).astype(jnp.float32)
        value = lefts[i]
        lanes = slice(i * LANES, (i + 1) * LANES)
        for j, part in enumerate((value * (1.0 - raised), value * raised)):
            high, low = split(part)
            lh[j * lines : (j + 1) * lines, lanes] = high
            ll[j * lines : (j + 1) * lines, lanes] = low


def close_pair(lh, ll, yh, yl, sigma, up, pair):
    sides = [jnp.concatenate([ref[2 * pair], ref[2 * pair + 1]], axis=1) for ref in (yh, yl)]
    both = fold((lh[...], ll[...]), sides)
    rows = both.shape[0] // 4
    sign = jnp.where(left_lanes((rows, LANES)), -1.0, 1.0)
    half = LANES // 2
    for j in range(2):
        for q in range(2):
            lanes = slice(q * LANES, (q + 1) * LANES)
            first = both[2 * j * rows : (2 * j + 1) * rows, lanes]
            second = both[(2 * j + 1) * rows : (2 * j + 2) * rows, lanes]
            value = (first + sign * turn(second)).T
            if j:
                up[0, 2 * pair + q], up[1, 2 * pair + q] = value[:half], value[half:]
            else:
                sigma[0, 2 * pair + q], sigma[1, 2 * pair + q] = value[:half], value[half:]


def whole_kernel(
    charge_hbm, source_hbm, coupling_hbm, owner_hbm, wave_ref, right_ref, left_ref, site_ref, sigma_hbm, new_hbm,
    charge_ref, source_ref, coupling_ref, owner_ref, site, wf, wloc, wh, wl, rv, pack, ops, tiles, lefts, sigma_ref, new_ref, rh, rl, dd, gh, gl, xa, xb, yh, yl, qs, lh, ll, nb, n1, n2, up, moved,
    out_sem, local, small_sem, wave_sem, first_s, first_l, far_s, far_l, near_s, near_l, last_s, last_l,
    tile_s, tile_l, left_s, left_l, twin_s, twin_l, n1_s, n1_l, n2_s, n2_l, up_s, up_l,
):
    ring = Ring()
    me, band = ring.me, ring.band
    slots = ops.shape[0]
    rows = LANES
    phys = yh.shape[0]
    flat = wh.shape[1]
    steps = wave_sem.shape[0]
    chunk = flat // steps

    load_right = pltpu.make_async_copy(right_ref, rv, local.at[0])
    load_right.start()
    load_site = pltpu.make_async_copy(site_ref, site, local.at[3])
    load_site.start()
    smalls = []
    for i, (source, target) in enumerate(
        ((charge_hbm, charge_ref), (source_hbm, source_ref), (coupling_hbm, coupling_ref), (owner_hbm, owner_ref))
    ):
        smalls.append(pltpu.make_async_copy(source, target, small_sem.at[i]))
        smalls[-1].start()
    lanes = pl.ds(pl.multiple_of(ring.z * LANES, LANES), LANES)
    loads = []
    for i in range(steps):
        part = pl.ds(i * chunk, chunk)
        loads.append(pltpu.make_async_copy(wave_ref.at[:, part, :], wf.at[i % 2], wave_sem.at[i]))
    load_local = pltpu.make_async_copy(wave_ref.at[:, :, lanes], wloc, local.at[1])
    load_left = pltpu.make_async_copy(left_ref, lefts.at[0], local.at[2])

    others = [lax.rem(band + i, 4) for i in range(1, 4)]
    places = [(ring.peer(i), band) for i in range(1, slots)] + [(me, other) for other in others]
    barrier = pltpu.get_barrier_semaphore()
    for place in places:
        pl.semaphore_signal(barrier, inc=1, device_id=place, device_id_type=pl.DeviceIdType.MESH)

    def first(i):
        other = lax.rem(i, 2)
        source = pack.at[i // 2, ring.y + other * (1 - 2 * ring.y), band]
        return remote(source, ops.at[i, band], first_s.at[i - 1], first_l.at[i - 1], (ring.peer(i), band))

    def far(i):
        block = ops.at[i, band]
        return remote(block, block, far_s.at[i - 1], far_l.at[i - 1], (me, ring.far))

    def near(i):
        block = ops.at[i, band]
        return remote(block, block, near_s.at[i - 1], near_l.at[i - 1], (me, ring.near))

    def last(i):
        block = ops.at[i, ring.far]
        return remote(block, block, last_s.at[i - 1], last_l.at[i - 1], (me, ring.near))

    def tile(i):
        return remote(tiles.at[0], tiles.at[i], tile_s.at[i - 1], tile_l.at[i - 1], (ring.peer(i), band))

    def over(j):
        return remote(left_ref, lefts.at[2 * j], left_s.at[j - 1], left_l.at[j - 1], (2 * ring.z_of(j) + ring.y, band))

    def twin(j):
        source = lefts.at[2 * j] if j else left_ref
        return remote(source, lefts.at[2 * j + 1], twin_s.at[j], twin_l.at[j], (ring.peer(1), band))

    load_right.wait()
    load_local.start()
    for load in loads[:2]:
        load.start()
    load_left.start()
    keep = pltpu.make_async_copy(pack.at[0, ring.y], ops.at[0], local.at[4])
    for j in range(slots // 2):
        pack_pair(rv, pack, j, ring.zs[j])
        if j == 0:
            keep.start()
            pl.semaphore_wait(barrier, len(places))
            first(1).start()
        elif j < 3:
            first(2 * j).start()
            first(2 * j + 1).start()
    load_site.wait()
    tiles[0] = jnp.concatenate([site[...]] * (LANES // phys), axis=1)
    for i in range(1, slots):
        tile(i).start()

    def forward(i):
        first(i).wait_recv()
        far(i).start()
        near(i).start()

    load_local.wait()
    local_weights(wloc, gh, gl, ring.y, phys, 0, phys // 2)
    for i in range(1, 4):
        forward(i)
    first(6).start()
    first(7).start()
    twin(0).start()
    for i in range(steps):
        loads[i].wait()
        split_rows(wf, wh, wl, i % 2, i * chunk)
        if i + 2 < steps:
            loads[i + 2].start()
    for i in range(1, 4):
        far(i).wait_recv()
        last(i).start()
    local_weights(wloc, gh, gl, ring.y, phys, phys // 2, phys)
    for i in range(1, slots):
        tile(i).wait_recv()
    site_blocks(tiles, dd)
    keep.wait()
    for i in range(1, 4):
        near(i).wait_recv()
        last(i).wait_recv()
    right_planes(ops, rh, rl, 0)

    height = flat // 4

    def make(step, xs):
        act_rows(wh, wl, rh, rl, xs, step, height)

    def use(step, xs):
        site_rows(dd, xs, yh, yl, step, phys, rows)

    order = (2, 3, 1, 0)

    def fold_one(j, half):
        sem = 4 * half + j
        return remote(nb.at[2 * j + 1, half], n1.at[j, half], n1_s.at[sem], n1_l.at[sem], (ring.peer(1), band))

    def fold_two(j, half):
        sem = 3 * half + j - 1
        return remote(nb.at[2 * j, half], n2.at[j - 1, half], n2_s.at[sem], n2_l.at[sem], (ring.peer(2 * j), band))

    def news(half):
        part = rows // 2
        overlaps(yh, yl, gh, gl, qs, [(i * rows + half * part, part) for i in range(4, 8)])
        for j in order:
            new_part(source_ref, coupling_ref, owner_ref, qs, nb, 2 * j + 1, half, ring, rows)
            fold_one(j, half).start()
        for j in order:
            new_part(source_ref, coupling_ref, owner_ref, qs, nb, 2 * j, half, ring, rows)

    def gather_news(j, half):
        fold_one(j, half).wait_recv()
        nb[2 * j, half] += n1[j, half]
        if j:
            fold_two(j, half).start()

    forward(4)
    forward(5)

    def act_two(u, carry):
        @pl.when(u == 1)
        def _():
            forward(6)
            forward(7)
            for i in range(4, 6):
                far(i).wait_recv()
                last(i).start()
            for j in (2, 3, 1):
                over(j).start()

        @pl.when(u == 2)
        def _():
            for i in range(6, 8):
                far(i).wait_recv()
                last(i).start()
            overlaps(yh, yl, gh, gl, qs, [(0, 4 * rows)])
            for i in range(4, 8):
                near(i).wait_recv()
                last(i).wait_recv()
            right_planes(ops, rh, rl, 1)
            over(1).wait_recv()
            twin(1).start()

        @pl.when(u == 3)
        def _():
            for j in range(2, 4):
                over(j).wait_recv()
                twin(j).start()
            news(0)

        make(2 * u, xa)
        make(2 * u + 1, xb)
        use(2 * u, xa)
        use(2 * u + 1, xb)
        return carry

    for small in smalls:
        small.wait()
    lax.fori_loop(0, 4, act_two, 0)
    news(1)
    for j in order:
        gather_news(j, 0)
    load_left.wait()
    for j in range(4):
        twin(j).wait_recv()
    left_stack(charge_ref, lefts, lh, ll, ring)

    above = lax.rem(band + 1, 4)

    def lift(pair):
        part = pl.ds(2 * pair, 2)
        return remote(up.at[:, part], moved.at[:, part], up_s.at[pair], up_l.at[pair], (me, above))

    def close_step(pair, carry):
        close_pair(lh, ll, yh, yl, sigma_ref, up, pair)

        @pl.when(band < 3)
        def _():
            lift(pair).start()

        for at, j in zip((1, 3, 5, 7), order):
            @pl.when(pair == at)
            def _():
                gather_news(j, 1)

        return carry

    lax.fori_loop(0, phys // 2, close_step, 0)

    def store(pair):
        part = pl.ds(2 * pair, 2)
        return pltpu.make_async_copy(sigma_ref.at[:, part], sigma_hbm.at[:, part], out_sem.at[pair])

    def gain(pair, carry):
        @pl.when(band > 0)
        def _():
            lift(pair).wait_recv()
            part = pl.ds(2 * pair, 2)
            sigma_ref[:, part] += moved[:, part]

        store(pair).start()
        return carry

    lax.fori_loop(0, phys // 2, gain, 0)
    for half in range(2):
        for j in order[:3]:
            fold_two(j, half).wait_recv()
        for part in range(2):
            total = nb[0, half, part]
            for j in order[:3]:
                total = total + n2[j - 1, half, part]
            start = part * rows + half * (rows // 2)
            new_ref[start : start + rows // 2, :] = total
    store_new = pltpu.make_async_copy(new_ref, new_hbm, out_sem.at[phys // 2])
    store_new.start()

    for i in range(1, slots):
        for copy in (first(i), far(i), near(i), last(i), tile(i)):
            copy.wait_send()
    for j in range(4):
        twin(j).wait_send()
        if j:
            over(j).wait_send()
        for half in range(2):
            fold_one(j, half).wait_send()
            if j:
                fold_two(j, half).wait_send()

    @pl.when(band < 3)
    def _():
        for pair in range(phys // 2):
            lift(pair).wait_send()

    store_new.wait()
    for pair in range(phys // 2):
        store(pair).wait()


def whole(charge, source, coupling, owner, wave, right, left, site):
    _, flat, bond = wave.shape
    terms = charge.shape[0]
    phys = site.shape[1]
    cols = bond // terms
    rows = flat // phys
    lines = terms * rows
    f32, bf16 = jnp.float32, jnp.bfloat16
    hbm = pl.BlockSpec(memory_space=pl.ANY)
    dma = lambda n: pltpu.SemaphoreType.DMA((n,))
    return pl.pallas_call(
        whole_kernel,
        in_specs=[hbm] * 8,
        out_specs=[hbm] * 2,
        out_shape=[
            jax.ShapeDtypeStruct((2, phys, cols, rows), f32),
            jax.ShapeDtypeStruct((2 * rows, rows), f32),
        ],
        scratch_shapes=[
            pltpu.SMEM(charge.shape, jnp.int32),
            pltpu.SMEM(source.shape, jnp.int32),
            pltpu.SMEM(coupling.shape, f32),
            pltpu.SMEM(owner.shape, jnp.int32),
            pltpu.VMEM(site.shape, f32),
            pltpu.VMEM((2, 2, flat // 4, bond), f32),
            pltpu.VMEM((2, flat, LANES), f32),
            pltpu.VMEM((3, flat, bond), bf16),
            pltpu.VMEM((3, flat, bond), bf16),
            pltpu.VMEM(right.shape, f32),
            pltpu.VMEM((terms // 2, 2, 4, bond // 4, LANES), f32),
            pltpu.VMEM((terms, 4, bond // 4, LANES), f32),
            pltpu.VMEM((terms, 2 * phys, LANES), f32),
            pltpu.VMEM((terms,) + left.shape, f32),
            pltpu.VMEM((2, phys, cols, rows), f32),
            pltpu.VMEM((2 * rows, rows), f32),
            pltpu.VMEM((2, 3, bond, 2 * LANES), bf16),
            pltpu.VMEM((2, 3, bond, 2 * LANES), bf16),
            pltpu.VMEM((terms, 16 * phys, 16 * phys), bf16),
            pltpu.VMEM((flat, 2 * rows), bf16),
            pltpu.VMEM((flat, 2 * rows), bf16),
            pltpu.VMEM((4, 2, 2, flat // 4, LANES), bf16),
            pltpu.VMEM((4, 2, 2, flat // 4, LANES), bf16),
            pltpu.VMEM((phys, lines, LANES), bf16),
            pltpu.VMEM((phys, lines, LANES), bf16),
            pltpu.VMEM((lines, 2 * LANES), f32),
            pltpu.VMEM((4 * rows, lines), bf16),
            pltpu.VMEM((4 * rows, lines), bf16),
            pltpu.VMEM((terms, 2, 2, rows // 2, rows), f32),
            pltpu.VMEM((terms // 2, 2, 2, rows // 2, rows), f32),
            pltpu.VMEM((terms // 2 - 1, 2, 2, rows // 2, rows), f32),
            pltpu.VMEM((2, phys, cols, rows), f32),
            pltpu.VMEM((2, phys, cols, rows), f32),
            dma(phys // 2 + 1),
            dma(5),
            dma(4),
            dma(4),
        ]
        + [dma(terms - 1)] * 10
        + [dma(terms // 2 - 1)] * 2
        + [dma(terms // 2)] * 2
        + [dma(terms)] * 2
        + [dma(terms - 2)] * 2
        + [dma(phys // 2)] * 2,
        compiler_params=pltpu.CompilerParams(
            collective_id=2, has_side_effects=True, vmem_limit_bytes=56 * 1024 * 1024
        ),
    )(charge, source, coupling, owner, wave, right, left, site)


def hand_kernel(sigma_ref, new_ref, sigma_out, new_out, sigma_mid, new_mid, ins, outs):
    parts = outs.shape[0] - 1
    width = sigma_ref.shape[1] // parts
    places = [(new_ref, new_mid, new_out)]
    for i in range(parts):
        part = pl.ds(i * width, width)
        places.append((sigma_ref.at[:, part], sigma_mid.at[:, part], sigma_out.at[:, part]))
    loads = [pltpu.make_async_copy(a, b, ins.at[i]) for i, (a, b, _) in enumerate(places)]
    stores = [pltpu.make_async_copy(b, c, outs.at[i]) for i, (_, b, c) in enumerate(places)]
    for load in loads:
        load.start()
    for load, store in zip(loads, stores):
        load.wait()
        store.start()
    for store in stores:
        store.wait()


def hand(sigma, new):
    spec = [pl.BlockSpec(memory_space=pl.ANY)] * 2
    return pl.pallas_call(
        hand_kernel,
        in_specs=spec,
        out_specs=spec,
        out_shape=[jax.ShapeDtypeStruct(v.shape, v.dtype) for v in (sigma, new)],
        scratch_shapes=[pltpu.VMEM(v.shape, v.dtype) for v in (sigma, new)] + [pltpu.SemaphoreType.DMA((5,))] * 2,
        compiler_params=pltpu.CompilerParams(vmem_limit_bytes=60 * 1024 * 1024),
    )(sigma, new)


def block(wave, left, right, site, charge, source, coupling, owner):
    _, rows, phys, bond = wave.shape
    sigma, new = whole(
        charge,
        source.T,
        coupling.transpose(2, 0, 1),
        owner,
        wave.reshape(2, rows * phys, bond),
        right[0],
        left[0].reshape(2 * rows, rows),
        site[0].reshape(2 * phys, phys),
    )
    sigma, new = hand(sigma, new)
    return sigma.transpose(0, 3, 1, 2), new.reshape(1, 2, rows, rows)


def body(wave, left, right, site, charge, source, coupling, owner):
    _, rows, phys, bond = wave.shape
    terms = lax.axis_size("terms")
    bands = lax.axis_size("sect")
    me = lax.axis_index("terms")
    cols = bond // terms
    per = LANES // cols
    pack = packed(right[0], terms).reshape(terms, bands, -1, LANES)
    lines = site.size // LANES
    room = -lines % 8
    small = jnp.concatenate(
        (left[0].reshape(2 * rows, rows), site.reshape(lines, LANES), jnp.zeros((room, LANES), jnp.float32))
    )
    ops, smalls = gather(pack, small)
    sites = smalls[:, 2 * rows : 2 * rows + lines].reshape(terms // per, per, 2, phys, phys)
    weights = jnp.stack((sites[:, :, 0], sites[:, :, 1], sites[:, :, 0] + sites[:, :, 1]))
    slot = jnp.arange(LANES, dtype=jnp.int32) // cols
    coef = sum(jnp.where(slot == j, weights[:, :, j, :, :, None], 0.0) for j in range(per))
    y = act(wave.reshape(2, rows * phys, bond), ops.reshape(terms, 2, bond // per, LANES), coef, phys)
    local = lax.dynamic_slice_in_dim(wave, me * cols, cols, axis=3).reshape(2 * rows, phys * cols)
    term_ids = jnp.arange(terms, dtype=jnp.int32)
    hit = (source[:, :, None] == term_ids).astype(jnp.float32)
    place = (owner[None, :] == term_ids[:, None]).astype(jnp.float32)
    weight = jnp.sum(coupling[:, :, :, None] * hit, axis=2)
    weight = jnp.sum(place[None, :, :, None] * weight[:, None], axis=2)
    stay, up, part = close(charge, weight, y, smalls, local)
    sigma, new = finish(stay, up, part)
    return sigma.reshape(2, rows, phys, cols), new.reshape(1, 2, rows, rows)


def solution(mesh):
    placed = (
        P(None, "sect", None, None),
        P("terms", None, "sect", None),
        P("terms", None, None, None),
        P("terms", None, None, None),
        P(),
        P(),
        P(),
        P(),
    )
    fits = mesh.shape["terms"] == 8 and mesh.shape["sect"] == 4
    return jax.shard_map(
        block if fits else body,
        mesh=mesh,
        in_specs=placed,
        out_specs=(P(None, "sect", None, "terms"), P("terms", None, "sect", None)),
        check_vma=False,
    )
```

```python
import functools

import jax
import jax.numpy as jnp
from jax import lax
from jax.experimental import pallas as pl
from jax.experimental.pallas import tpu as pltpu
from jax.sharding import PartitionSpec as P

LANES = 128


def split(value):
    high = value.astype(jnp.bfloat16)
    return high, (value - high.astype(jnp.float32)).astype(jnp.bfloat16)


def triple(former, latter, dims=(((1,), (0,)), ((), ()))):
    dot = functools.partial(lax.dot_general, dimension_numbers=dims, preferred_element_type=jnp.float32)
    return dot(former[0], latter[0]) + dot(former[0], latter[1]) + dot(former[1], latter[0])


def act_kernel(wave_ref, ops_ref, coef_ref, y_ref, high, low, mixed):
    groups, _, phys, rows, _ = y_ref.shape

    @pl.when(pl.program_id(0) == 0)
    def _():
        per = ops_ref.shape[0] // groups
        cols = LANES // per
        deep = ops_ref.shape[2]
        for g in range(groups):
            lanes = slice(g * LANES, (g + 1) * LANES)
            for i in range(per):
                part = [
                    jnp.concatenate(
                        [ops_ref[g * per + j, h, :, i * cols : (i + 1) * cols] for j in range(per)], axis=1
                    )
                    for h in range(2)
                ]
                for j, value in enumerate((part[0], part[1], part[0] + part[1])):
                    spot = (j, slice(i * deep, (i + 1) * deep), lanes)
                    high[spot], low[spot] = split(value)

    re, im = wave_ref[0], wave_ref[1]
    t = [triple(split(v), (high[j], low[j])) for j, v in enumerate((re, im, re + im))]
    for j, value in enumerate((t[0] - t[1], t[2] - t[0] - t[1], t[2] - 2.0 * t[1])):
        for g in range(groups):
            mixed[j, g] = value[:, g * LANES : (g + 1) * LANES]

    def block(step, carry):
        g, r = step // (rows // 8), step % (rows // 8)
        base = pl.multiple_of(r * 8 * phys, 8 * phys)
        x = [[mixed[j, g, pl.ds(base + q, 8, stride=phys), :] for q in range(phys)] for j in range(3)]
        out = pl.ds(pl.multiple_of(r * 8, 8), 8)
        for p in range(phys):
            s = []
            for j in range(3):
                total = coef_ref[j, g, p, 0:1, :] * x[j][0]
                for q in range(1, phys):
                    total = total + coef_ref[j, g, p, q : q + 1, :] * x[j][q]
                s.append(total)
            y_ref[g, 0, p, out, :] = s[0] - s[1]
            y_ref[g, 1, p, out, :] = s[2] - s[0] - s[1]
        return carry

    lax.fori_loop(0, groups * (rows // 8), block, 0)


def act(wave, ops, coef, phys):
    _, flat, bond = wave.shape
    rows = flat // phys
    groups = coef.shape[1]
    width = groups * LANES
    step = 32
    return pl.pallas_call(
        act_kernel,
        grid=(rows // step,),
        in_specs=[
            pl.BlockSpec((2, step * phys, bond), lambda i: (0, i, 0)),
            pl.BlockSpec(ops.shape, lambda i: (0, 0, 0, 0)),
            pl.BlockSpec(coef.shape, lambda i: (0, 0, 0, 0, 0)),
        ],
        out_specs=pl.BlockSpec((groups, 2, phys, step, LANES), lambda i: (0, 0, 0, i, 0)),
        out_shape=jax.ShapeDtypeStruct((groups, 2, phys, rows, LANES), jnp.float32),
        scratch_shapes=[
            pltpu.VMEM((3, bond, width), jnp.bfloat16),
            pltpu.VMEM((3, bond, width), jnp.bfloat16),
            pltpu.VMEM((3, groups, step * phys, LANES), jnp.float32),
        ],
        compiler_params=pltpu.CompilerParams(vmem_limit_bytes=58 * 1024 * 1024),
    )(wave, ops, coef)


def close_kernel(charge_ref, weight_ref, y_ref, left_ref, local_ref, stay_ref, up_ref, new_ref, high, low):
    per = left_ref.shape[0]
    terms = new_ref.shape[0]
    phys, rows = y_ref.shape[2], y_ref.shape[3]
    cols = LANES // per
    group = pl.program_id(0)

    @pl.when(group == 0)
    def _():
        high[...], low[...] = split(local_ref[...])
        stay_ref[...] = jnp.zeros_like(stay_ref)
        up_ref[...] = jnp.zeros_like(up_ref)
        new_ref[...] = jnp.zeros_like(new_ref)

    for j in range(per):
        term = group * per + j
        y = jnp.concatenate(
            [
                jnp.concatenate([y_ref[0, h, p, :, j * cols : (j + 1) * cols] for p in range(phys)], axis=1)
                for h in range(2)
            ],
            axis=0,
        )
        y = split(y)
        re, im = left_ref[j, :rows], left_ref[j, rows : 2 * rows]
        left = jnp.concatenate(
            [jnp.concatenate([re, -im], axis=1), jnp.concatenate([im, re], axis=1)], axis=0
        )
        c = triple(split(left), y)
        raised = (charge_ref[term] == 1).astype(jnp.float32)
        up_ref[...] += c * raised
        stay_ref[...] += c * (1.0 - raised)
        gram = triple(y, (high[...], low[...]), (((1,), (1,)), ((), ())))
        q_re = gram[:rows, :rows] + gram[rows:, rows:]
        q_im = gram[rows:, :rows] - gram[:rows, rows:]

        def add(g, carry):
            w_re, w_im = weight_ref[0, g, term], weight_ref[1, g, term]
            new_ref[g, :rows, :] += w_re * q_re - w_im * q_im
            new_ref[g, rows:, :] += w_re * q_im + w_im * q_re
            return carry

        lax.fori_loop(0, terms, add, 0)


def close(charge, weight, y, left, local):
    groups, _, phys, rows, _ = y.shape
    terms, lines, _ = left.shape
    per = terms // groups
    tall, wide = local.shape
    fixed = pl.BlockSpec((tall, wide), lambda i: (0, 0))
    return pl.pallas_call(
        close_kernel,
        grid=(groups,),
        in_specs=[
            pl.BlockSpec(memory_space=pltpu.SMEM),
            pl.BlockSpec(memory_space=pltpu.SMEM),
            pl.BlockSpec((1, 2, phys, rows, LANES), lambda i: (i, 0, 0, 0, 0)),
            pl.BlockSpec((per, lines, rows), lambda i: (i, 0, 0)),
            fixed,
        ],
        out_specs=[pl.BlockSpec(memory_space=pltpu.VMEM)] * 3,
        out_shape=[
            jax.ShapeDtypeStruct((tall, wide), jnp.float32),
            jax.ShapeDtypeStruct((tall, wide), jnp.float32),
            jax.ShapeDtypeStruct((terms, tall, rows), jnp.float32),
        ],
        scratch_shapes=[pltpu.VMEM((tall, wide), jnp.bfloat16)] * 2,
        compiler_params=pltpu.CompilerParams(vmem_limit_bytes=54 * 1024 * 1024),
    )(charge, weight, y, left, local)


def pack_kernel(right_ref, pack_ref):
    terms, _, deep, _ = pack_ref.shape
    cols = right_ref.shape[2] // terms
    per = LANES // cols
    for t in range(terms):
        for h in range(2):
            pieces = [right_ref[h, i * deep : (i + 1) * deep, t * cols : (t + 1) * cols] for i in range(per)]
            pack_ref[t, h] = jnp.concatenate(pieces, axis=1)


def packed(right, terms):
    _, bond, width = right.shape
    deep = bond * width // (terms * LANES)
    vmem = pl.BlockSpec(memory_space=pltpu.VMEM)
    return pl.pallas_call(
        pack_kernel,
        in_specs=[vmem],
        out_specs=vmem,
        out_shape=jax.ShapeDtypeStruct((terms, 2, deep, LANES), jnp.float32),
        compiler_params=pltpu.CompilerParams(vmem_limit_bytes=16 * 1024 * 1024),
    )(right)


def remote(source, target, sends, lands, place):
    return pltpu.make_async_remote_copy(
        src_ref=source,
        dst_ref=target,
        send_sem=sends,
        recv_sem=lands,
        device_id=place,
        device_id_type=pl.DeviceIdType.MESH,
    )


def greet(places):
    barrier = pltpu.get_barrier_semaphore()
    for place in places:
        pl.semaphore_signal(barrier, inc=1, device_id=place, device_id_type=pl.DeviceIdType.MESH)
    pl.semaphore_wait(barrier, len(places))


def gather_kernel(pack_ref, small_ref, ops_ref, smalls_ref, send_a, land_a, send_x, land_x, send_c, land_c, send_f, land_f, send_s, land_s, send_t, land_t, own):
    terms, bands = pack_ref.shape[:2]
    half = terms // 2
    me = lax.axis_index("terms")
    band = lax.axis_index("sect")
    twin = me + 1 - 2 * lax.rem(me, 2)
    near = band + 1 - 2 * lax.rem(band, 2)
    far = lax.rem(band + 2, 4)
    greet([(lax.rem(me + i, terms), band) for i in range(1, terms)] + [(me, near), (me, far)])
    keep = pltpu.make_async_copy(pack_ref.at[me], ops_ref.at[me], own.at[0])
    keep.start()
    keep_small = pltpu.make_async_copy(small_ref, smalls_ref.at[me], own.at[1])
    keep_small.start()
    first = []
    for i in range(1, terms):
        peer = lax.rem(me + i, terms)
        copy = remote(pack_ref.at[peer, band], ops_ref.at[me, band], send_a.at[i - 1], land_a.at[i - 1], (peer, band))
        copy.start()
        first.append(copy)
    tiny = []
    for i in range(half):
        place = (twin if i == 0 else lax.rem(me + 2 * i, terms), band)
        copy = remote(small_ref, smalls_ref.at[me], send_s.at[i], land_s.at[i], place)
        copy.start()
        tiny.append(copy)
    across, beside = [], []
    for i in range(1, terms):
        first[i - 1].wait_recv()
        block = ops_ref.at[lax.rem(me + terms - i, terms), band]
        copy = remote(block, block, send_x.at[i - 1], land_x.at[i - 1], (me, far))
        copy.start()
        across.append(copy)
        copy = remote(block, block, send_c.at[i - 1], land_c.at[i - 1], (me, near))
        copy.start()
        beside.append(copy)
    relay = []
    for i in range(1, half):
        tiny[i].wait_recv()
        block = smalls_ref.at[lax.rem(me + terms - 2 * i, terms)]
        copy = remote(block, block, send_t.at[i - 1], land_t.at[i - 1], (twin, band))
        copy.start()
        relay.append(copy)
    last = []
    for i in range(1, terms):
        across[i - 1].wait_recv()
        block = ops_ref.at[lax.rem(me + terms - i, terms), far]
        copy = remote(block, block, send_f.at[i - 1], land_f.at[i - 1], (me, near))
        copy.start()
        last.append(copy)
    for copy in beside + last + relay + tiny[:1]:
        copy.wait_recv()
    for copy in first + tiny + across + beside + relay + last:
        copy.wait_send()
    keep.wait()
    keep_small.wait()


def gather(pack, small):
    terms = pack.shape[0]
    vmem = pl.BlockSpec(memory_space=pltpu.VMEM)
    pair = [pltpu.SemaphoreType.DMA((terms - 1,))] * 2
    return pl.pallas_call(
        gather_kernel,
        in_specs=[vmem, vmem],
        out_specs=[vmem, vmem],
        out_shape=[
            jax.ShapeDtypeStruct(pack.shape, jnp.float32),
            jax.ShapeDtypeStruct((terms,) + small.shape, jnp.float32),
        ],
        scratch_shapes=pair * 6 + [pltpu.SemaphoreType.DMA((2,))],
        compiler_params=pltpu.CompilerParams(
            collective_id=0, has_side_effects=True, vmem_limit_bytes=24 * 1024 * 1024
        ),
    )(pack, small)


def finish_kernel(stay_ref, up_ref, part_ref, sigma_ref, new_ref, moved, got, held, mine, send_a, land_a, edge):
    terms = part_ref.shape[0]
    me = lax.axis_index("terms")
    band = lax.axis_index("sect")
    bands = lax.axis_size("sect")
    upper = lax.rem(band + 1, bands)
    lower = lax.rem(band + bands - 1, bands)
    greet([(lax.rem(me + i, terms), band) for i in range(1, terms)] + [(me, upper), (me, lower)])
    shift = remote(up_ref, moved, edge.at[0], edge.at[1], (me, upper))
    shift.start()
    copies = []
    for i in range(1, terms):
        peer = lax.rem(me + i, terms)
        copy = remote(part_ref.at[peer], got.at[i - 1], send_a.at[i - 1], land_a.at[i - 1], (peer, band))
        copy.start()
        copies.append(copy)
    keep = pltpu.make_async_copy(stay_ref, held, edge.at[2])
    keep.start()
    keep_part = pltpu.make_async_copy(part_ref.at[me], mine, edge.at[3])
    keep_part.start()
    keep.wait()
    keep_part.wait()
    shift.wait()
    sigma_ref[...] = held[...] + jnp.where(band > 0, moved[...], 0.0)
    total = mine[...]
    for i, copy in enumerate(copies):
        copy.wait()
        total = total + got[i]
    new_ref[...] = total


def finish(stay, up, part):
    terms = part.shape[0]
    vmem = pl.BlockSpec(memory_space=pltpu.VMEM)
    return pl.pallas_call(
        finish_kernel,
        in_specs=[pl.BlockSpec(memory_space=pl.ANY)] * 3,
        out_specs=[vmem] * 2,
        out_shape=[
            jax.ShapeDtypeStruct(stay.shape, jnp.float32),
            jax.ShapeDtypeStruct(part.shape[1:], jnp.float32),
        ],
        scratch_shapes=[
            pltpu.VMEM(stay.shape, jnp.float32),
            pltpu.VMEM((terms - 1,) + part.shape[1:], jnp.float32),
            pltpu.VMEM(stay.shape, jnp.float32),
            pltpu.VMEM(part.shape[1:], jnp.float32),
            pltpu.SemaphoreType.DMA((terms - 1,)),
            pltpu.SemaphoreType.DMA((terms - 1,)),
            pltpu.SemaphoreType.DMA((4,)),
        ],
        compiler_params=pltpu.CompilerParams(
            collective_id=1, has_side_effects=True, vmem_limit_bytes=24 * 1024 * 1024
        ),
    )(stay, up, part)


def fold(value, other):
    dot = functools.partial(jnp.dot, preferred_element_type=jnp.float32)
    return dot(value[0], other[0]) + dot(value[0], other[1]) + dot(value[1], other[0])


def turn(value):
    return pltpu.roll(value, LANES // 2, 1)


def left_lanes(shape):
    return lax.broadcasted_iota(jnp.int32, shape, 1) < LANES // 2


class Ring:
    def __init__(self):
        self.me = lax.axis_index("terms")
        self.band = lax.axis_index("sect")
        self.z, self.y = self.me // 2, lax.rem(self.me, 2)
        flip = 1 - 2 * lax.rem(self.z, 2)
        self.zs = [self.z, self.z + flip, lax.rem(self.z + 2, 4), 3 - self.z]
        self.near = self.band + 1 - 2 * lax.rem(self.band, 2)
        self.far = lax.rem(self.band + 2, 4)

    def z_of(self, pair):
        if isinstance(pair, int):
            return self.zs[pair]
        low, high = lax.rem(pair, 2), pair // 2
        here = self.z + low * (self.zs[1] - self.z)
        there = self.zs[2] + low * (self.zs[3] - self.zs[2])
        return here + high * (there - here)

    def peer(self, slot):
        pair, other = slot // 2, slot % 2 if isinstance(slot, int) else lax.rem(slot, 2)
        y = self.y + other * (1 - 2 * self.y)
        return 2 * self.z_of(pair) + y


def split_rows(wf, wh, wl, slot, start):
    re, im = wf[slot, 0], wf[slot, 1]
    rows = pl.ds(start, re.shape[0])
    for j, value in enumerate((re, im, re + im)):
        high, low = split(value)
        wh[j, rows, :] = high
        wl[j, rows, :] = low


def pack_pair(rv, pack, pair, place):
    deep = rv.shape[1] // 2
    lanes = pl.ds(pl.multiple_of(place * LANES, LANES), LANES)
    for h in range(2):
        for part in range(2):
            half = deep // 2
            top = rv[h, part * half : (part + 1) * half, lanes]
            low = rv[h, deep + part * half : deep + (part + 1) * half, lanes]
            left = left_lanes(top.shape)
            pack[pair, 0, 2 * h + part] = jnp.where(left, top, turn(low))
            pack[pair, 1, 2 * h + part] = jnp.where(left, turn(top), low)


def local_weights(wloc, gh, gl, odd, phys, start, end):
    rows = wloc.shape[1] // phys

    def one(p, carry):
        re = wloc[0, pl.ds(p, rows, stride=phys), :]
        im = wloc[1, pl.ds(p, rows, stride=phys), :]
        left = left_lanes(re.shape)
        even_value = jnp.where(left, re, turn(im))
        odd_value = jnp.where(left, turn(re), im)
        value = jnp.where(odd == 0, even_value, odd_value).T
        half = LANES // 2
        both = jnp.concatenate([value, jnp.concatenate([-value[half:], value[:half]], axis=0)], axis=1)
        high, low = split(both)
        out = pl.ds(pl.multiple_of(p * LANES, LANES), LANES)
        gh[out, :] = high
        gl[out, :] = low
        return carry

    lax.fori_loop(start, end, one, 0)


def site_blocks(tiles, dd):
    slots, lines, _ = tiles.shape
    group = 8

    def one(i, carry):
        value = jnp.broadcast_to(tiles[i][:, None, :], (lines, group, LANES))
        column = lax.broadcasted_iota(jnp.int32, value.shape, 2) // (LANES // group)
        row = lax.broadcasted_iota(jnp.int32, value.shape, 1)
        value = jnp.where(column == row, value, 0.0).reshape(lines * group, LANES)
        half = lines * group // 2
        high, low = split(jnp.concatenate([value[:half], value[half:]], axis=1))
        dd[i, :half, :] = high
        dd[i, half:, :] = low
        return carry

    lax.fori_loop(0, slots, one, 0)


def right_planes(ops, rh, rl, batch):
    deep = ops.shape[2]
    for pair in range(2):
        first = batch * 4 + 2 * pair
        lanes = slice(pair * LANES, (pair + 1) * LANES)
        for part in range(2):
            tops, lows = [], []
            for h in range(2):
                a, b = ops[first, 2 * h + part], ops[first + 1, 2 * h + part]
                left = left_lanes(a.shape)
                tops.append(jnp.where(left, a, turn(b)))
                lows.append(jnp.where(left, turn(a), b))
            for offset, (re, im) in ((part * deep, tops), ((2 + part) * deep, lows)):
                for j, value in enumerate((re, im, re + im)):
                    high, low = split(value)
                    rh[batch, j, offset : offset + deep, lanes] = high
                    rl[batch, j, offset : offset + deep, lanes] = low


def act_rows(wh, wl, rh, rl, xs, step, height):
    batch = step // 4
    rows = pl.ds(pl.multiple_of(lax.rem(step, 4) * height, height), height)
    t = [fold((wh[j, rows, :], wl[j, rows, :]), (rh[batch, j], rl[batch, j])) for j in range(3)]
    re, im = t[0] - t[1], t[2] - t[0] - t[1]
    for pair in range(2):
        lanes = slice(pair * LANES, (pair + 1) * LANES)
        a, b = re[:, lanes], im[:, lanes]
        at, bt = turn(a), turn(b)
        left = left_lanes(a.shape)
        xs[2 * pair, 0, 0], xs[2 * pair, 0, 1] = split(jnp.where(left, a, bt))
        xs[2 * pair, 1, 0], xs[2 * pair, 1, 1] = split(jnp.where(left, -b, at))
        xs[2 * pair + 1, 0, 0], xs[2 * pair + 1, 0, 1] = split(jnp.where(left, at, b))
        xs[2 * pair + 1, 1, 0], xs[2 * pair + 1, 1, 1] = split(jnp.where(left, -bt, a))


def site_rows(dd, xs, yh, yl, step, phys):
    dot = functools.partial(jnp.dot, preferred_element_type=jnp.float32)
    height = xs.shape[3]
    deep = 8 * phys
    base = lax.rem(step, 4) * (height // phys)
    for i in range(4):
        slot = (step // 4) * 4 + i
        for g in range(height // (2 * deep)):
            one, two = g * 2 * deep, (g * 2 + 1) * deep
            sides = [
                jnp.concatenate(
                    [
                        jnp.concatenate([xs[i, j, h, one : one + deep], xs[i, j, h, two : two + deep]], axis=1)
                        for j in range(2)
                    ],
                    axis=0,
                )
                for h in range(2)
            ]
            wide = dot(dd[slot], sides[0])
            y = wide[:deep] + wide[deep:] + dot(dd[slot, :deep], sides[1])
            y = jnp.concatenate(
                [y[:, :LANES].reshape(phys, 8, LANES), y[:, LANES:].reshape(phys, 8, LANES)], axis=1
            )
            high, low = split(y)
            out = pl.ds(pl.multiple_of(base + g * 16, 16), 16)
            yh[:, slot, out, :] = high
            yl[:, slot, out, :] = low


def overlaps(yh, yl, gh, gl, qs, slots, part):
    phys, rows = yh.shape[0], yh.shape[2]
    wide = [
        jnp.concatenate([jnp.concatenate([ref[p, i, part, :] for i in slots], axis=0) for p in range(phys)], axis=1)
        for ref in (yh, yl)
    ]
    value = fold(wide, (gh[...], gl[...]))
    count = part.stop - part.start
    for n, i in enumerate(slots):
        qs[i * rows + part.start : i * rows + part.stop, :] = value[n * count : (n + 1) * count]


def new_part(source_ref, coupling_ref, owner_ref, qs, nb, slot, half, ring, rows):
    target = ring.peer(slot)
    slots, top = owner_ref.shape[0], source_ref.shape[0]
    fresh = jnp.int32(0)
    for j in range(1, slots):
        fresh = jnp.where(owner_ref[j] == target, j, fresh)
    sources = [source_ref[t, fresh] for t in range(top)]
    factors = [(coupling_ref[t, 0, fresh], coupling_ref[t, 1, fresh]) for t in range(top)]
    count = rows // 2
    re = jnp.zeros((count, LANES), jnp.float32)
    im = jnp.zeros((count, LANES), jnp.float32)
    for i in range(slots):
        term = ring.peer(i)
        w_re, w_im = jnp.float32(0.0), jnp.float32(0.0)
        for term_t, (f_re, f_im) in zip(sources, factors):
            w_re = w_re + jnp.where(term_t == term, f_re, 0.0)
            w_im = w_im + jnp.where(term_t == term, f_im, 0.0)
        part = slice(i * rows + half * count, i * rows + (half + 1) * count)
        q_re, q_im = qs[part, :LANES], qs[part, LANES:]
        re = re + (w_re * q_re - w_im * q_im)
        im = im + (w_re * q_im + w_im * q_re)
    nb[slot, half, 0] = re
    nb[slot, half, 1] = im


def by_charge(charge_ref, ring, slots):
    raised = [charge_ref[ring.peer(i)] for i in range(slots)]
    ups = sum(raised[1:], raised[0])
    places, up, stay = [], jnp.int32(0), ups + lax.rem(ups, 2)
    for flag in raised:
        places.append(jnp.where(flag == 1, up, stay))
        up, stay = up + flag, stay + 1 - flag
    entries = []
    for e in range(slots + 2):
        slot, used = jnp.int32(0), jnp.float32(0.0)
        for i, place in enumerate(places):
            slot = jnp.where(place == e, i, slot)
            used = jnp.where(place == e, 1.0, used)
        entries.append((slot, used))
    flags = [jnp.where(2 * t < ups, 1.0, 0.0) for t in range(slots // 2 + 1)]
    return entries, flags


def left_stack(lefts, lh, ll, entries):
    for e, (slot, used) in enumerate(entries):
        lanes = slice(e * LANES, (e + 1) * LANES)
        lh[:, lanes], ll[:, lanes] = split(lefts[slot] * used)


def close_pair(lh, ll, yh, yl, sigma, up, pair, entries, flags):
    rows = lh.shape[0] // 2
    total, lifted = None, None
    for t, flag in enumerate(flags):
        lanes = slice(2 * t * rows, (2 * t + 2) * rows)
        spots = [entries[2 * t + i][0] for i in range(2)]
        sides = [
            jnp.concatenate(
                [jnp.concatenate([ref[2 * pair, spot], ref[2 * pair + 1, spot]], axis=1) for spot in spots],
                axis=0,
            )
            for ref in (yh, yl)
        ]
        value = fold((lh[:, lanes], ll[:, lanes]), sides)
        part = value * flag
        value = value * (1.0 - flag)
        total = value if total is None else total + value
        lifted = part if lifted is None else lifted + part
    sign = jnp.where(left_lanes((rows, LANES)), -1.0, 1.0)
    half = LANES // 2
    for target, value in ((sigma, total), (up, lifted)):
        for q in range(2):
            lanes = slice(q * LANES, (q + 1) * LANES)
            out = (value[:rows, lanes] + sign * turn(value[rows:, lanes])).T
            target[0, 2 * pair + q], target[1, 2 * pair + q] = out[:half], out[half:]


def whole_kernel(
    charge_hbm, source_hbm, coupling_hbm, owner_hbm, wave_ref, right_ref, left_ref, site_ref, sigma_hbm, new_hbm,
    charge_ref, source_ref, coupling_ref, owner_ref, site, wf, wloc, wh, wl, rv, pack, ops, tiles, lefts, sigma_ref, new_ref, rh, rl, dd, gh, gl, xa, xb, yh, yl, qs, lh, ll, nb, n1, n2, up, moved,
    out_sem, local, small_sem, wave_sem, first_s, first_l, far_s, far_l, near_s, near_l, last_s, last_l,
    tile_s, tile_l, left_s, left_l, twin_s, twin_l, n1_s, n1_l, n2_s, n2_l, up_s, up_l,
):
    ring = Ring()
    me, band = ring.me, ring.band
    slots = ops.shape[0]
    rows = LANES
    phys = yh.shape[0]
    flat = wh.shape[1]
    steps = wave_sem.shape[0]
    chunk = flat // steps

    load_right = pltpu.make_async_copy(right_ref, rv, local.at[0])
    load_right.start()
    load_site = pltpu.make_async_copy(site_ref, site, local.at[3])
    load_site.start()
    smalls = []
    for i, (source, target) in enumerate(
        ((charge_hbm, charge_ref), (source_hbm, source_ref), (coupling_hbm, coupling_ref), (owner_hbm, owner_ref))
    ):
        smalls.append(pltpu.make_async_copy(source, target, small_sem.at[i]))
        smalls[-1].start()
    lanes = pl.ds(pl.multiple_of(ring.z * LANES, LANES), LANES)
    loads = []
    for i in range(steps):
        part = pl.ds(i * chunk, chunk)
        loads.append(pltpu.make_async_copy(wave_ref.at[:, part, :], wf.at[i % 2], wave_sem.at[i]))
    load_local = pltpu.make_async_copy(wave_ref.at[:, :, lanes], wloc, local.at[1])
    load_left = pltpu.make_async_copy(left_ref, lefts.at[0], local.at[2])

    others = [lax.rem(band + i, 4) for i in range(1, 4)]
    places = [(ring.peer(i), band) for i in range(1, slots)] + [(me, other) for other in others]
    barrier = pltpu.get_barrier_semaphore()
    for place in places:
        pl.semaphore_signal(barrier, inc=1, device_id=place, device_id_type=pl.DeviceIdType.MESH)

    def first(i):
        other = lax.rem(i, 2)
        source = pack.at[i // 2, ring.y + other * (1 - 2 * ring.y), band]
        return remote(source, ops.at[i, band], first_s.at[i - 1], first_l.at[i - 1], (ring.peer(i), band))

    def far(i):
        block = ops.at[i, band]
        return remote(block, block, far_s.at[i - 1], far_l.at[i - 1], (me, ring.far))

    def near(i):
        block = ops.at[i, band]
        return remote(block, block, near_s.at[i - 1], near_l.at[i - 1], (me, ring.near))

    def last(i):
        block = ops.at[i, ring.far]
        return remote(block, block, last_s.at[i - 1], last_l.at[i - 1], (me, ring.near))

    def tile(i):
        return remote(tiles.at[0], tiles.at[i], tile_s.at[i - 1], tile_l.at[i - 1], (ring.peer(i), band))

    def over(j):
        source, step = (lefts.at[4], 1) if j == 3 else (left_ref, j)
        return remote(source, lefts.at[2 * j], left_s.at[j - 1], left_l.at[j - 1], (ring.peer(2 * step), band))

    def twin(j):
        source = lefts.at[2 * j] if j else left_ref
        return remote(source, lefts.at[2 * j + 1], twin_s.at[j], twin_l.at[j], (ring.peer(1), band))

    load_right.wait()
    load_local.start()
    for load in loads[:2]:
        load.start()
    load_left.start()
    keep = pltpu.make_async_copy(pack.at[0, ring.y], ops.at[0], local.at[4])
    for j in range(slots // 2):
        pack_pair(rv, pack, j, ring.zs[j])
        if j == 0:
            keep.start()
            pl.semaphore_wait(barrier, len(places))
            first(1).start()
        elif j < 3:
            first(2 * j).start()
            first(2 * j + 1).start()
    load_site.wait()
    tiles[0] = jnp.concatenate([site[...]] * (LANES // phys), axis=1)
    for i in range(1, slots):
        tile(i).start()

    def forward(i):
        first(i).wait_recv()
        far(i).start()
        near(i).start()

    load_local.wait()
    local_weights(wloc, gh, gl, ring.y, phys, 0, phys // 2)
    for i in range(1, 4):
        forward(i)
    first(6).start()
    first(7).start()
    twin(0).start()
    over(1).start()
    for i in range(steps):
        loads[i].wait()
        split_rows(wf, wh, wl, i % 2, i * chunk)
        if i + 2 < steps:
            loads[i + 2].start()
    for i in range(1, 4):
        far(i).wait_recv()
        last(i).start()
    local_weights(wloc, gh, gl, ring.y, phys, phys // 2, phys)
    for i in range(1, slots):
        tile(i).wait_recv()
    site_blocks(tiles, dd)
    keep.wait()
    for i in range(1, 4):
        near(i).wait_recv()
        last(i).wait_recv()
    right_planes(ops, rh, rl, 0)

    height = flat // 4

    def make(step, xs):
        act_rows(wh, wl, rh, rl, xs, step, height)

    def use(step, xs):
        site_rows(dd, xs, yh, yl, step, phys)

    order = (2, 3, 1, 0)

    def fold_one(j, half):
        sem = 4 * half + j
        return remote(nb.at[2 * j + 1, half], n1.at[j, half], n1_s.at[sem], n1_l.at[sem], (ring.peer(1), band))

    def fold_two(j, half):
        sem = 3 * half + j - 1
        return remote(nb.at[2 * j, half], n2.at[j - 1, half], n2_s.at[sem], n2_l.at[sem], (ring.peer(2 * j), band))

    def news(half):
        part = rows // 2
        overlaps(yh, yl, gh, gl, qs, range(4, 8), slice(half * part, (half + 1) * part))
        for j in order:
            new_part(source_ref, coupling_ref, owner_ref, qs, nb, 2 * j + 1, half, ring, rows)
            fold_one(j, half).start()
        for j in order:
            new_part(source_ref, coupling_ref, owner_ref, qs, nb, 2 * j, half, ring, rows)

    def gather_news(j, half):
        fold_one(j, half).wait_recv()
        nb[2 * j, half] += n1[j, half]
        if j:
            fold_two(j, half).start()

    forward(4)
    forward(5)

    def act_two(u, carry):
        @pl.when(u == 1)
        def _():
            forward(6)
            forward(7)
            for i in range(4, 6):
                far(i).wait_recv()
                last(i).start()
            over(2).start()
            over(1).wait_recv()
            twin(1).start()

        @pl.when(u == 2)
        def _():
            for i in range(6, 8):
                far(i).wait_recv()
                last(i).start()
            overlaps(yh, yl, gh, gl, qs, range(4), slice(0, rows))
            for i in range(4, 8):
                near(i).wait_recv()
                last(i).wait_recv()
            right_planes(ops, rh, rl, 1)
            over(2).wait_recv()
            over(3).start()
            twin(2).start()

        @pl.when(u == 3)
        def _():
            over(3).wait_recv()
            twin(3).start()
            news(0)

        make(2 * u, xa)
        make(2 * u + 1, xb)
        use(2 * u, xa)
        use(2 * u + 1, xb)
        return carry

    for small in smalls:
        small.wait()
    lax.fori_loop(0, 4, act_two, 0)
    news(1)
    load_left.wait()
    for j in range(4):
        twin(j).wait_recv()
    entries, flags = by_charge(charge_ref, ring, slots)
    left_stack(lefts, lh, ll, entries)

    above = lax.rem(band + 1, 4)

    def lift(pair):
        part = pl.ds(2 * pair, 2)
        return remote(up.at[:, part], moved.at[:, part], up_s.at[pair], up_l.at[pair], (me, above))

    def close_step(step, carry):
        for at, j in enumerate(order):
            @pl.when(step == at // 2)
            def _():
                gather_news(j, 0)

            @pl.when(step == at // 2 + 2)
            def _():
                gather_news(j, 1)

        for pair in (2 * step, 2 * step + 1):
            close_pair(lh, ll, yh, yl, sigma_ref, up, pair, entries, flags)

        @pl.when(band < 3)
        def _():
            lift(2 * step).start()
            lift(2 * step + 1).start()

        return carry

    lax.fori_loop(0, phys // 4, close_step, 0)

    def store(pair):
        part = pl.ds(2 * pair, 2)
        return pltpu.make_async_copy(sigma_ref.at[:, part], sigma_hbm.at[:, part], out_sem.at[pair])

    def gain(pair, carry):
        @pl.when(band > 0)
        def _():
            lift(pair).wait_recv()
            part = pl.ds(2 * pair, 2)
            sigma_ref[:, part] += moved[:, part]

        store(pair).start()
        return carry

    lax.fori_loop(0, phys // 2, gain, 0)
    for half in range(2):
        for j in order[:3]:
            fold_two(j, half).wait_recv()
        for part in range(2):
            total = nb[0, half, part]
            for j in order[:3]:
                total = total + n2[j - 1, half, part]
            start = part * rows + half * (rows // 2)
            new_ref[start : start + rows // 2, :] = total
    store_new = pltpu.make_async_copy(new_ref, new_hbm, out_sem.at[phys // 2])
    store_new.start()

    for i in range(1, slots):
        for copy in (first(i), far(i), near(i), last(i), tile(i)):
            copy.wait_send()
    for j in range(4):
        twin(j).wait_send()
        if j:
            over(j).wait_send()
        for half in range(2):
            fold_one(j, half).wait_send()
            if j:
                fold_two(j, half).wait_send()

    @pl.when(band < 3)
    def _():
        for pair in range(phys // 2):
            lift(pair).wait_send()

    store_new.wait()
    for pair in range(phys // 2):
        store(pair).wait()


def whole(charge, source, coupling, owner, wave, right, left, site):
    _, flat, bond = wave.shape
    terms = charge.shape[0]
    phys = site.shape[1]
    cols = bond // terms
    rows = flat // phys
    lines = terms * rows
    f32, bf16 = jnp.float32, jnp.bfloat16
    hbm = pl.BlockSpec(memory_space=pl.ANY)
    dma = lambda n: pltpu.SemaphoreType.DMA((n,))
    return pl.pallas_call(
        whole_kernel,
        in_specs=[hbm] * 8,
        out_specs=[hbm] * 2,
        out_shape=[
            jax.ShapeDtypeStruct((2, phys, cols, rows), f32),
            jax.ShapeDtypeStruct((2 * rows, rows), f32),
        ],
        scratch_shapes=[
            pltpu.SMEM(charge.shape, jnp.int32),
            pltpu.SMEM(source.shape, jnp.int32),
            pltpu.SMEM(coupling.shape, f32),
            pltpu.SMEM(owner.shape, jnp.int32),
            pltpu.VMEM(site.shape, f32),
            pltpu.VMEM((2, 2, flat // 4, bond), f32),
            pltpu.VMEM((2, flat, LANES), f32),
            pltpu.VMEM((3, flat, bond), bf16),
            pltpu.VMEM((3, flat, bond), bf16),
            pltpu.VMEM(right.shape, f32),
            pltpu.VMEM((terms // 2, 2, 4, bond // 4, LANES), f32),
            pltpu.VMEM((terms, 4, bond // 4, LANES), f32),
            pltpu.VMEM((terms, 2 * phys, LANES), f32),
            pltpu.VMEM((terms,) + left.shape, f32),
            pltpu.VMEM((2, phys, cols, rows), f32),
            pltpu.VMEM((2 * rows, rows), f32),
            pltpu.VMEM((2, 3, bond, 2 * LANES), bf16),
            pltpu.VMEM((2, 3, bond, 2 * LANES), bf16),
            pltpu.VMEM((terms, 16 * phys, 16 * phys), bf16),
            pltpu.VMEM((flat, 2 * rows), bf16),
            pltpu.VMEM((flat, 2 * rows), bf16),
            pltpu.VMEM((4, 2, 2, flat // 4, LANES), bf16),
            pltpu.VMEM((4, 2, 2, flat // 4, LANES), bf16),
            pltpu.VMEM((phys, terms, rows, LANES), bf16),
            pltpu.VMEM((phys, terms, rows, LANES), bf16),
            pltpu.VMEM((lines, 2 * LANES), f32),
            pltpu.VMEM((2 * rows, lines + 2 * rows), bf16),
            pltpu.VMEM((2 * rows, lines + 2 * rows), bf16),
            pltpu.VMEM((terms, 2, 2, rows // 2, rows), f32),
            pltpu.VMEM((terms // 2, 2, 2, rows // 2, rows), f32),
            pltpu.VMEM((terms // 2 - 1, 2, 2, rows // 2, rows), f32),
            pltpu.VMEM((2, phys, cols, rows), f32),
            pltpu.VMEM((2, phys, cols, rows), f32),
            dma(phys // 2 + 1),
            dma(5),
            dma(4),
            dma(4),
        ]
        + [dma(terms - 1)] * 10
        + [dma(terms // 2 - 1)] * 2
        + [dma(terms // 2)] * 2
        + [dma(terms)] * 2
        + [dma(terms - 2)] * 2
        + [dma(phys // 2)] * 2,
        compiler_params=pltpu.CompilerParams(
            collective_id=2, has_side_effects=True, vmem_limit_bytes=56 * 1024 * 1024
        ),
    )(charge, source, coupling, owner, wave, right, left, site)


def hand_kernel(sigma_ref, new_ref, sigma_out, new_out, sigma_mid, new_mid, ins, outs):
    parts = outs.shape[0] - 1
    width = sigma_ref.shape[1] // parts
    places = [(new_ref, new_mid, new_out)]
    for i in range(parts):
        part = pl.ds(i * width, width)
        places.append((sigma_ref.at[:, part], sigma_mid.at[:, part], sigma_out.at[:, part]))
    loads = [pltpu.make_async_copy(a, b, ins.at[i]) for i, (a, b, _) in enumerate(places)]
    stores = [pltpu.make_async_copy(b, c, outs.at[i]) for i, (_, b, c) in enumerate(places)]
    for load in loads:
        load.start()
    for load, store in zip(loads, stores):
        load.wait()
        store.start()
    for store in stores:
        store.wait()


def hand(sigma, new):
    spec = [pl.BlockSpec(memory_space=pl.ANY)] * 2
    return pl.pallas_call(
        hand_kernel,
        in_specs=spec,
        out_specs=spec,
        out_shape=[jax.ShapeDtypeStruct(v.shape, v.dtype) for v in (sigma, new)],
        scratch_shapes=[pltpu.VMEM(v.shape, v.dtype) for v in (sigma, new)] + [pltpu.SemaphoreType.DMA((5,))] * 2,
        compiler_params=pltpu.CompilerParams(vmem_limit_bytes=60 * 1024 * 1024),
    )(sigma, new)


def block(wave, left, right, site, charge, source, coupling, owner):
    _, rows, phys, bond = wave.shape
    sigma, new = whole(
        charge,
        source.T,
        coupling.transpose(2, 0, 1),
        owner,
        wave.reshape(2, rows * phys, bond),
        right[0],
        left[0].reshape(2 * rows, rows),
        site[0].reshape(2 * phys, phys),
    )
    sigma, new = hand(sigma, new)
    return sigma.transpose(0, 3, 1, 2), new.reshape(1, 2, rows, rows)


def body(wave, left, right, site, charge, source, coupling, owner):
    _, rows, phys, bond = wave.shape
    terms = lax.axis_size("terms")
    bands = lax.axis_size("sect")
    me = lax.axis_index("terms")
    cols = bond // terms
    per = LANES // cols
    pack = packed(right[0], terms).reshape(terms, bands, -1, LANES)
    lines = site.size // LANES
    room = -lines % 8
    small = jnp.concatenate(
        (left[0].reshape(2 * rows, rows), site.reshape(lines, LANES), jnp.zeros((room, LANES), jnp.float32))
    )
    ops, smalls = gather(pack, small)
    sites = smalls[:, 2 * rows : 2 * rows + lines].reshape(terms // per, per, 2, phys, phys)
    weights = jnp.stack((sites[:, :, 0], sites[:, :, 1], sites[:, :, 0] + sites[:, :, 1]))
    slot = jnp.arange(LANES, dtype=jnp.int32) // cols
    coef = sum(jnp.where(slot == j, weights[:, :, j, :, :, None], 0.0) for j in range(per))
    y = act(wave.reshape(2, rows * phys, bond), ops.reshape(terms, 2, bond // per, LANES), coef, phys)
    local = lax.dynamic_slice_in_dim(wave, me * cols, cols, axis=3).reshape(2 * rows, phys * cols)
    term_ids = jnp.arange(terms, dtype=jnp.int32)
    hit = (source[:, :, None] == term_ids).astype(jnp.float32)
    place = (owner[None, :] == term_ids[:, None]).astype(jnp.float32)
    weight = jnp.sum(coupling[:, :, :, None] * hit, axis=2)
    weight = jnp.sum(place[None, :, :, None] * weight[:, None], axis=2)
    stay, up, part = close(charge, weight, y, smalls, local)
    sigma, new = finish(stay, up, part)
    return sigma.reshape(2, rows, phys, cols), new.reshape(1, 2, rows, rows)


def solution(mesh):
    placed = (
        P(None, "sect", None, None),
        P("terms", None, "sect", None),
        P("terms", None, None, None),
        P("terms", None, None, None),
        P(),
        P(),
        P(),
        P(),
    )
    fits = mesh.shape["terms"] == 8 and mesh.shape["sect"] == 4
    return jax.shard_map(
        block if fits else body,
        mesh=mesh,
        in_specs=placed,
        out_specs=(P(None, "sect", None, "terms"), P("terms", None, "sect", None)),
        check_vma=False,
    )
```

```python
import functools

import jax
import jax.numpy as jnp
from jax import lax
from jax.experimental import pallas as pl
from jax.experimental.pallas import tpu as pltpu
from jax.sharding import PartitionSpec as P

LANES = 128


def split(value):
    high = value.astype(jnp.bfloat16)
    return high, (value - high.astype(jnp.float32)).astype(jnp.bfloat16)


def triple(former, latter, dims=(((1,), (0,)), ((), ()))):
    dot = functools.partial(lax.dot_general, dimension_numbers=dims, preferred_element_type=jnp.float32)
    return dot(former[0], latter[0]) + dot(former[0], latter[1]) + dot(former[1], latter[0])


def act_kernel(wave_ref, ops_ref, coef_ref, y_ref, high, low, mixed):
    groups, _, phys, rows, _ = y_ref.shape

    @pl.when(pl.program_id(0) == 0)
    def _():
        per = ops_ref.shape[0] // groups
        cols = LANES // per
        deep = ops_ref.shape[2]
        for g in range(groups):
            lanes = slice(g * LANES, (g + 1) * LANES)
            for i in range(per):
                part = [
                    jnp.concatenate(
                        [ops_ref[g * per + j, h, :, i * cols : (i + 1) * cols] for j in range(per)], axis=1
                    )
                    for h in range(2)
                ]
                for j, value in enumerate((part[0], part[1], part[0] + part[1])):
                    spot = (j, slice(i * deep, (i + 1) * deep), lanes)
                    high[spot], low[spot] = split(value)

    re, im = wave_ref[0], wave_ref[1]
    t = [triple(split(v), (high[j], low[j])) for j, v in enumerate((re, im, re + im))]
    for j, value in enumerate((t[0] - t[1], t[2] - t[0] - t[1], t[2] - 2.0 * t[1])):
        for g in range(groups):
            mixed[j, g] = value[:, g * LANES : (g + 1) * LANES]

    def block(step, carry):
        g, r = step // (rows // 8), step % (rows // 8)
        base = pl.multiple_of(r * 8 * phys, 8 * phys)
        x = [[mixed[j, g, pl.ds(base + q, 8, stride=phys), :] for q in range(phys)] for j in range(3)]
        out = pl.ds(pl.multiple_of(r * 8, 8), 8)
        for p in range(phys):
            s = []
            for j in range(3):
                total = coef_ref[j, g, p, 0:1, :] * x[j][0]
                for q in range(1, phys):
                    total = total + coef_ref[j, g, p, q : q + 1, :] * x[j][q]
                s.append(total)
            y_ref[g, 0, p, out, :] = s[0] - s[1]
            y_ref[g, 1, p, out, :] = s[2] - s[0] - s[1]
        return carry

    lax.fori_loop(0, groups * (rows // 8), block, 0)


def act(wave, ops, coef, phys):
    _, flat, bond = wave.shape
    rows = flat // phys
    groups = coef.shape[1]
    width = groups * LANES
    step = 32
    return pl.pallas_call(
        act_kernel,
        grid=(rows // step,),
        in_specs=[
            pl.BlockSpec((2, step * phys, bond), lambda i: (0, i, 0)),
            pl.BlockSpec(ops.shape, lambda i: (0, 0, 0, 0)),
            pl.BlockSpec(coef.shape, lambda i: (0, 0, 0, 0, 0)),
        ],
        out_specs=pl.BlockSpec((groups, 2, phys, step, LANES), lambda i: (0, 0, 0, i, 0)),
        out_shape=jax.ShapeDtypeStruct((groups, 2, phys, rows, LANES), jnp.float32),
        scratch_shapes=[
            pltpu.VMEM((3, bond, width), jnp.bfloat16),
            pltpu.VMEM((3, bond, width), jnp.bfloat16),
            pltpu.VMEM((3, groups, step * phys, LANES), jnp.float32),
        ],
        compiler_params=pltpu.CompilerParams(vmem_limit_bytes=58 * 1024 * 1024),
    )(wave, ops, coef)


def close_kernel(charge_ref, weight_ref, y_ref, left_ref, local_ref, stay_ref, up_ref, new_ref, high, low):
    per = left_ref.shape[0]
    terms = new_ref.shape[0]
    phys, rows = y_ref.shape[2], y_ref.shape[3]
    cols = LANES // per
    group = pl.program_id(0)

    @pl.when(group == 0)
    def _():
        high[...], low[...] = split(local_ref[...])
        stay_ref[...] = jnp.zeros_like(stay_ref)
        up_ref[...] = jnp.zeros_like(up_ref)
        new_ref[...] = jnp.zeros_like(new_ref)

    for j in range(per):
        term = group * per + j
        y = jnp.concatenate(
            [
                jnp.concatenate([y_ref[0, h, p, :, j * cols : (j + 1) * cols] for p in range(phys)], axis=1)
                for h in range(2)
            ],
            axis=0,
        )
        y = split(y)
        re, im = left_ref[j, :rows], left_ref[j, rows : 2 * rows]
        left = jnp.concatenate(
            [jnp.concatenate([re, -im], axis=1), jnp.concatenate([im, re], axis=1)], axis=0
        )
        c = triple(split(left), y)
        raised = (charge_ref[term] == 1).astype(jnp.float32)
        up_ref[...] += c * raised
        stay_ref[...] += c * (1.0 - raised)
        gram = triple(y, (high[...], low[...]), (((1,), (1,)), ((), ())))
        q_re = gram[:rows, :rows] + gram[rows:, rows:]
        q_im = gram[rows:, :rows] - gram[:rows, rows:]

        def add(g, carry):
            w_re, w_im = weight_ref[0, g, term], weight_ref[1, g, term]
            new_ref[g, :rows, :] += w_re * q_re - w_im * q_im
            new_ref[g, rows:, :] += w_re * q_im + w_im * q_re
            return carry

        lax.fori_loop(0, terms, add, 0)


def close(charge, weight, y, left, local):
    groups, _, phys, rows, _ = y.shape
    terms, lines, _ = left.shape
    per = terms // groups
    tall, wide = local.shape
    fixed = pl.BlockSpec((tall, wide), lambda i: (0, 0))
    return pl.pallas_call(
        close_kernel,
        grid=(groups,),
        in_specs=[
            pl.BlockSpec(memory_space=pltpu.SMEM),
            pl.BlockSpec(memory_space=pltpu.SMEM),
            pl.BlockSpec((1, 2, phys, rows, LANES), lambda i: (i, 0, 0, 0, 0)),
            pl.BlockSpec((per, lines, rows), lambda i: (i, 0, 0)),
            fixed,
        ],
        out_specs=[pl.BlockSpec(memory_space=pltpu.VMEM)] * 3,
        out_shape=[
            jax.ShapeDtypeStruct((tall, wide), jnp.float32),
            jax.ShapeDtypeStruct((tall, wide), jnp.float32),
            jax.ShapeDtypeStruct((terms, tall, rows), jnp.float32),
        ],
        scratch_shapes=[pltpu.VMEM((tall, wide), jnp.bfloat16)] * 2,
        compiler_params=pltpu.CompilerParams(vmem_limit_bytes=54 * 1024 * 1024),
    )(charge, weight, y, left, local)


def pack_kernel(right_ref, pack_ref):
    terms, _, deep, _ = pack_ref.shape
    cols = right_ref.shape[2] // terms
    per = LANES // cols
    for t in range(terms):
        for h in range(2):
            pieces = [right_ref[h, i * deep : (i + 1) * deep, t * cols : (t + 1) * cols] for i in range(per)]
            pack_ref[t, h] = jnp.concatenate(pieces, axis=1)


def packed(right, terms):
    _, bond, width = right.shape
    deep = bond * width // (terms * LANES)
    vmem = pl.BlockSpec(memory_space=pltpu.VMEM)
    return pl.pallas_call(
        pack_kernel,
        in_specs=[vmem],
        out_specs=vmem,
        out_shape=jax.ShapeDtypeStruct((terms, 2, deep, LANES), jnp.float32),
        compiler_params=pltpu.CompilerParams(vmem_limit_bytes=16 * 1024 * 1024),
    )(right)


def remote(source, target, sends, lands, place):
    return pltpu.make_async_remote_copy(
        src_ref=source,
        dst_ref=target,
        send_sem=sends,
        recv_sem=lands,
        device_id=place,
        device_id_type=pl.DeviceIdType.MESH,
    )


def greet(places):
    barrier = pltpu.get_barrier_semaphore()
    for place in places:
        pl.semaphore_signal(barrier, inc=1, device_id=place, device_id_type=pl.DeviceIdType.MESH)
    pl.semaphore_wait(barrier, len(places))


def gather_kernel(pack_ref, small_ref, ops_ref, smalls_ref, send_a, land_a, send_x, land_x, send_c, land_c, send_f, land_f, send_s, land_s, send_t, land_t, own):
    terms, bands = pack_ref.shape[:2]
    half = terms // 2
    me = lax.axis_index("terms")
    band = lax.axis_index("sect")
    twin = me + 1 - 2 * lax.rem(me, 2)
    near = band + 1 - 2 * lax.rem(band, 2)
    far = lax.rem(band + 2, 4)
    greet([(lax.rem(me + i, terms), band) for i in range(1, terms)] + [(me, near), (me, far)])
    keep = pltpu.make_async_copy(pack_ref.at[me], ops_ref.at[me], own.at[0])
    keep.start()
    keep_small = pltpu.make_async_copy(small_ref, smalls_ref.at[me], own.at[1])
    keep_small.start()
    first = []
    for i in range(1, terms):
        peer = lax.rem(me + i, terms)
        copy = remote(pack_ref.at[peer, band], ops_ref.at[me, band], send_a.at[i - 1], land_a.at[i - 1], (peer, band))
        copy.start()
        first.append(copy)
    tiny = []
    for i in range(half):
        place = (twin if i == 0 else lax.rem(me + 2 * i, terms), band)
        copy = remote(small_ref, smalls_ref.at[me], send_s.at[i], land_s.at[i], place)
        copy.start()
        tiny.append(copy)
    across, beside = [], []
    for i in range(1, terms):
        first[i - 1].wait_recv()
        block = ops_ref.at[lax.rem(me + terms - i, terms), band]
        copy = remote(block, block, send_x.at[i - 1], land_x.at[i - 1], (me, far))
        copy.start()
        across.append(copy)
        copy = remote(block, block, send_c.at[i - 1], land_c.at[i - 1], (me, near))
        copy.start()
        beside.append(copy)
    relay = []
    for i in range(1, half):
        tiny[i].wait_recv()
        block = smalls_ref.at[lax.rem(me + terms - 2 * i, terms)]
        copy = remote(block, block, send_t.at[i - 1], land_t.at[i - 1], (twin, band))
        copy.start()
        relay.append(copy)
    last = []
    for i in range(1, terms):
        across[i - 1].wait_recv()
        block = ops_ref.at[lax.rem(me + terms - i, terms), far]
        copy = remote(block, block, send_f.at[i - 1], land_f.at[i - 1], (me, near))
        copy.start()
        last.append(copy)
    for copy in beside + last + relay + tiny[:1]:
        copy.wait_recv()
    for copy in first + tiny + across + beside + relay + last:
        copy.wait_send()
    keep.wait()
    keep_small.wait()


def gather(pack, small):
    terms = pack.shape[0]
    vmem = pl.BlockSpec(memory_space=pltpu.VMEM)
    pair = [pltpu.SemaphoreType.DMA((terms - 1,))] * 2
    return pl.pallas_call(
        gather_kernel,
        in_specs=[vmem, vmem],
        out_specs=[vmem, vmem],
        out_shape=[
            jax.ShapeDtypeStruct(pack.shape, jnp.float32),
            jax.ShapeDtypeStruct((terms,) + small.shape, jnp.float32),
        ],
        scratch_shapes=pair * 6 + [pltpu.SemaphoreType.DMA((2,))],
        compiler_params=pltpu.CompilerParams(
            collective_id=0, has_side_effects=True, vmem_limit_bytes=24 * 1024 * 1024
        ),
    )(pack, small)


def finish_kernel(stay_ref, up_ref, part_ref, sigma_ref, new_ref, moved, got, held, mine, send_a, land_a, edge):
    terms = part_ref.shape[0]
    me = lax.axis_index("terms")
    band = lax.axis_index("sect")
    bands = lax.axis_size("sect")
    upper = lax.rem(band + 1, bands)
    lower = lax.rem(band + bands - 1, bands)
    greet([(lax.rem(me + i, terms), band) for i in range(1, terms)] + [(me, upper), (me, lower)])
    shift = remote(up_ref, moved, edge.at[0], edge.at[1], (me, upper))
    shift.start()
    copies = []
    for i in range(1, terms):
        peer = lax.rem(me + i, terms)
        copy = remote(part_ref.at[peer], got.at[i - 1], send_a.at[i - 1], land_a.at[i - 1], (peer, band))
        copy.start()
        copies.append(copy)
    keep = pltpu.make_async_copy(stay_ref, held, edge.at[2])
    keep.start()
    keep_part = pltpu.make_async_copy(part_ref.at[me], mine, edge.at[3])
    keep_part.start()
    keep.wait()
    keep_part.wait()
    shift.wait()
    sigma_ref[...] = held[...] + jnp.where(band > 0, moved[...], 0.0)
    total = mine[...]
    for i, copy in enumerate(copies):
        copy.wait()
        total = total + got[i]
    new_ref[...] = total


def finish(stay, up, part):
    terms = part.shape[0]
    vmem = pl.BlockSpec(memory_space=pltpu.VMEM)
    return pl.pallas_call(
        finish_kernel,
        in_specs=[pl.BlockSpec(memory_space=pl.ANY)] * 3,
        out_specs=[vmem] * 2,
        out_shape=[
            jax.ShapeDtypeStruct(stay.shape, jnp.float32),
            jax.ShapeDtypeStruct(part.shape[1:], jnp.float32),
        ],
        scratch_shapes=[
            pltpu.VMEM(stay.shape, jnp.float32),
            pltpu.VMEM((terms - 1,) + part.shape[1:], jnp.float32),
            pltpu.VMEM(stay.shape, jnp.float32),
            pltpu.VMEM(part.shape[1:], jnp.float32),
            pltpu.SemaphoreType.DMA((terms - 1,)),
            pltpu.SemaphoreType.DMA((terms - 1,)),
            pltpu.SemaphoreType.DMA((4,)),
        ],
        compiler_params=pltpu.CompilerParams(
            collective_id=1, has_side_effects=True, vmem_limit_bytes=24 * 1024 * 1024
        ),
    )(stay, up, part)


def fold(value, other):
    dot = functools.partial(jnp.dot, preferred_element_type=jnp.float32)
    return dot(value[0], other[0]) + dot(value[0], other[1]) + dot(value[1], other[0])


def turn(value):
    return pltpu.roll(value, LANES // 2, 1)


def left_lanes(shape):
    return lax.broadcasted_iota(jnp.int32, shape, 1) < LANES // 2


class Ring:
    def __init__(self):
        self.me = lax.axis_index("terms")
        self.band = lax.axis_index("sect")
        self.z, self.y = self.me // 2, lax.rem(self.me, 2)
        flip = 1 - 2 * lax.rem(self.z, 2)
        self.zs = [self.z, self.z + flip, lax.rem(self.z + 2, 4), 3 - self.z]
        self.near = self.band + 1 - 2 * lax.rem(self.band, 2)
        self.far = lax.rem(self.band + 2, 4)

    def z_of(self, pair):
        if isinstance(pair, int):
            return self.zs[pair]
        low, high = lax.rem(pair, 2), pair // 2
        here = self.z + low * (self.zs[1] - self.z)
        there = self.zs[2] + low * (self.zs[3] - self.zs[2])
        return here + high * (there - here)

    def peer(self, slot):
        pair, other = slot // 2, slot % 2 if isinstance(slot, int) else lax.rem(slot, 2)
        y = self.y + other * (1 - 2 * self.y)
        return 2 * self.z_of(pair) + y


def split_rows(wf, wh, wl, slot, start):
    re, im = wf[slot, 0], wf[slot, 1]
    rows = pl.ds(start, re.shape[0])
    for j, value in enumerate((re, im, re + im)):
        high, low = split(value)
        wh[j, rows, :] = high
        wl[j, rows, :] = low


def pack_pair(rv, pack, pair, place):
    deep = rv.shape[1] // 2
    lanes = pl.ds(pl.multiple_of(place * LANES, LANES), LANES)
    for h in range(2):
        for part in range(2):
            half = deep // 2
            top = rv[h, part * half : (part + 1) * half, lanes]
            low = rv[h, deep + part * half : deep + (part + 1) * half, lanes]
            left = left_lanes(top.shape)
            pack[pair, 0, 2 * h + part] = jnp.where(left, top, turn(low))
            pack[pair, 1, 2 * h + part] = jnp.where(left, turn(top), low)


def local_weights(wloc, gh, gl, odd, phys, start, end):
    rows = wloc.shape[1] // phys

    def one(p, carry):
        re = wloc[0, pl.ds(p, rows, stride=phys), :]
        im = wloc[1, pl.ds(p, rows, stride=phys), :]
        left = left_lanes(re.shape)
        even_value = jnp.where(left, re, turn(im))
        odd_value = jnp.where(left, turn(re), im)
        value = jnp.where(odd == 0, even_value, odd_value).T
        half = LANES // 2
        both = jnp.concatenate([value, jnp.concatenate([-value[half:], value[:half]], axis=0)], axis=1)
        high, low = split(both)
        out = pl.ds(pl.multiple_of(p * LANES, LANES), LANES)
        gh[out, :] = high
        gl[out, :] = low
        return carry

    lax.fori_loop(start, end, one, 0)


def site_blocks(tiles, dd):
    slots, lines, _ = tiles.shape
    group = 8

    def one(i, carry):
        value = jnp.broadcast_to(tiles[i][:, None, :], (lines, group, LANES))
        column = lax.broadcasted_iota(jnp.int32, value.shape, 2) // (LANES // group)
        row = lax.broadcasted_iota(jnp.int32, value.shape, 1)
        value = jnp.where(column == row, value, 0.0).reshape(lines * group, LANES)
        half = lines * group // 2
        high, low = split(jnp.concatenate([value[:half], value[half:]], axis=1))
        dd[i, :half, :] = high
        dd[i, half:, :] = low
        return carry

    lax.fori_loop(0, slots, one, 0)


def right_planes(ops, rh, rl, batch):
    deep = ops.shape[2]
    for pair in range(2):
        first = batch * 4 + 2 * pair
        lanes = slice(pair * LANES, (pair + 1) * LANES)
        for part in range(2):
            tops, lows = [], []
            for h in range(2):
                a, b = ops[first, 2 * h + part], ops[first + 1, 2 * h + part]
                left = left_lanes(a.shape)
                tops.append(jnp.where(left, a, turn(b)))
                lows.append(jnp.where(left, turn(a), b))
            for offset, (re, im) in ((part * deep, tops), ((2 + part) * deep, lows)):
                for j, value in enumerate((re, im, re + im)):
                    high, low = split(value)
                    rh[batch, j, offset : offset + deep, lanes] = high
                    rl[batch, j, offset : offset + deep, lanes] = low


def act_rows(wh, wl, rh, rl, xs, step, height):
    batch = step // 4
    rows = pl.ds(pl.multiple_of(lax.rem(step, 4) * height, height), height)
    t = [fold((wh[j, rows, :], wl[j, rows, :]), (rh[batch, j], rl[batch, j])) for j in range(3)]
    re, im = t[0] - t[1], t[2] - t[0] - t[1]
    for pair in range(2):
        lanes = slice(pair * LANES, (pair + 1) * LANES)
        a, b = re[:, lanes], im[:, lanes]
        at, bt = turn(a), turn(b)
        left = left_lanes(a.shape)
        xs[2 * pair, 0, 0], xs[2 * pair, 0, 1] = split(jnp.where(left, a, bt))
        xs[2 * pair, 1, 0], xs[2 * pair, 1, 1] = split(jnp.where(left, -b, at))
        xs[2 * pair + 1, 0, 0], xs[2 * pair + 1, 0, 1] = split(jnp.where(left, at, b))
        xs[2 * pair + 1, 1, 0], xs[2 * pair + 1, 1, 1] = split(jnp.where(left, -bt, a))


def site_rows(dd, xs, yh, yl, step, phys):
    dot = functools.partial(jnp.dot, preferred_element_type=jnp.float32)
    height = xs.shape[3]
    deep = 8 * phys
    base = lax.rem(step, 4) * (height // phys)
    for i in range(4):
        slot = (step // 4) * 4 + i
        for g in range(height // (2 * deep)):
            one, two = g * 2 * deep, (g * 2 + 1) * deep
            sides = [
                jnp.concatenate(
                    [
                        jnp.concatenate([xs[i, j, h, one : one + deep], xs[i, j, h, two : two + deep]], axis=1)
                        for j in range(2)
                    ],
                    axis=0,
                )
                for h in range(2)
            ]
            wide = dot(dd[slot], sides[0])
            y = wide[:deep] + wide[deep:] + dot(dd[slot, :deep], sides[1])
            y = jnp.concatenate(
                [y[:, :LANES].reshape(phys, 8, LANES), y[:, LANES:].reshape(phys, 8, LANES)], axis=1
            )
            high, low = split(y)
            out = pl.ds(pl.multiple_of(base + g * 16, 16), 16)
            yh[:, slot, out, :] = high
            yl[:, slot, out, :] = low


def overlaps(yh, yl, gh, gl, qs, slots, part):
    phys, rows = yh.shape[0], yh.shape[2]
    wide = [
        jnp.concatenate([jnp.concatenate([ref[p, i, part, :] for i in slots], axis=0) for p in range(phys)], axis=1)
        for ref in (yh, yl)
    ]
    value = fold(wide, (gh[...], gl[...]))
    count = part.stop - part.start
    for n, i in enumerate(slots):
        qs[i * rows + part.start : i * rows + part.stop, :] = value[n * count : (n + 1) * count]


def new_part(source_ref, coupling_ref, owner_ref, qs, nb, slot, half, ring, rows):
    target = ring.peer(slot)
    slots, top = owner_ref.shape[0], source_ref.shape[0]
    fresh = jnp.int32(0)
    for j in range(1, slots):
        fresh = jnp.where(owner_ref[j] == target, j, fresh)
    sources = [source_ref[t, fresh] for t in range(top)]
    factors = [(coupling_ref[t, 0, fresh], coupling_ref[t, 1, fresh]) for t in range(top)]
    count = rows // 2
    re = jnp.zeros((count, LANES), jnp.float32)
    im = jnp.zeros((count, LANES), jnp.float32)
    for i in range(slots):
        term = ring.peer(i)
        w_re, w_im = jnp.float32(0.0), jnp.float32(0.0)
        for term_t, (f_re, f_im) in zip(sources, factors):
            w_re = w_re + jnp.where(term_t == term, f_re, 0.0)
            w_im = w_im + jnp.where(term_t == term, f_im, 0.0)
        part = slice(i * rows + half * count, i * rows + (half + 1) * count)
        q_re, q_im = qs[part, :LANES], qs[part, LANES:]
        re = re + (w_re * q_re - w_im * q_im)
        im = im + (w_re * q_im + w_im * q_re)
    nb[slot, half, 0] = re
    nb[slot, half, 1] = im


def by_charge(charge_ref, ring, slots):
    raised = [charge_ref[ring.peer(i)] for i in range(slots)]
    ups = sum(raised[1:], raised[0])
    places, up, stay = [], jnp.int32(0), ups + lax.rem(ups, 2)
    for flag in raised:
        places.append(jnp.where(flag == 1, up, stay))
        up, stay = up + flag, stay + 1 - flag
    entries = []
    for e in range(slots + 2):
        slot, used = jnp.int32(0), jnp.float32(0.0)
        for i, place in enumerate(places):
            slot = jnp.where(place == e, i, slot)
            used = jnp.where(place == e, 1.0, used)
        entries.append((slot, used))
    flags = [jnp.where(2 * t < ups, 1.0, 0.0) for t in range(slots // 2 + 1)]
    return entries, flags


def left_stack(lefts, lh, ll, entries):
    for e, (slot, used) in enumerate(entries):
        lanes = slice(e * LANES, (e + 1) * LANES)
        lh[:, lanes], ll[:, lanes] = split(lefts[slot] * used)


def close_pair(lh, ll, yh, yl, sigma, up, pair, entries, flags):
    rows = lh.shape[0] // 2
    total, lifted = None, None
    for t, flag in enumerate(flags):
        lanes = slice(2 * t * rows, (2 * t + 2) * rows)
        spots = [entries[2 * t + i][0] for i in range(2)]
        sides = [
            jnp.concatenate(
                [jnp.concatenate([ref[2 * pair, spot], ref[2 * pair + 1, spot]], axis=1) for spot in spots],
                axis=0,
            )
            for ref in (yh, yl)
        ]
        value = fold((lh[:, lanes], ll[:, lanes]), sides)
        part = value * flag
        value = value * (1.0 - flag)
        total = value if total is None else total + value
        lifted = part if lifted is None else lifted + part
    sign = jnp.where(left_lanes((rows, LANES)), -1.0, 1.0)
    half = LANES // 2
    for target, value in ((sigma, total), (up, lifted)):
        for q in range(2):
            lanes = slice(q * LANES, (q + 1) * LANES)
            out = (value[:rows, lanes] + sign * turn(value[rows:, lanes])).T
            target[0, 2 * pair + q], target[1, 2 * pair + q] = out[:half], out[half:]


def whole_kernel(
    charge_hbm, source_hbm, coupling_hbm, owner_hbm, wave_ref, right_ref, left_ref, site_ref, sigma_hbm, new_hbm,
    charge_ref, source_ref, coupling_ref, owner_ref, site, wf, wloc, wh, wl, rv, pack, ops, tiles, lefts, sigma_ref, new_ref, rh, rl, dd, gh, gl, xa, xb, yh, yl, qs, lh, ll, nb, n1, n2, up, moved,
    out_sem, local, small_sem, wave_sem, first_s, first_l, far_s, far_l, near_s, near_l, last_s, last_l,
    tile_s, tile_l, left_s, left_l, twin_s, twin_l, n1_s, n1_l, n2_s, n2_l, up_s, up_l,
):
    ring = Ring()
    me, band = ring.me, ring.band
    slots = ops.shape[0]
    rows = LANES
    phys = yh.shape[0]
    flat = wh.shape[1]
    steps = wave_sem.shape[0]
    chunk = flat // steps

    load_right = pltpu.make_async_copy(right_ref, rv, local.at[0])
    load_right.start()
    load_site = pltpu.make_async_copy(site_ref, site, local.at[3])
    load_site.start()
    smalls = []
    for i, (source, target) in enumerate(
        ((charge_hbm, charge_ref), (source_hbm, source_ref), (coupling_hbm, coupling_ref), (owner_hbm, owner_ref))
    ):
        smalls.append(pltpu.make_async_copy(source, target, small_sem.at[i]))
        smalls[-1].start()
    lanes = pl.ds(pl.multiple_of(ring.z * LANES, LANES), LANES)
    loads = []
    for i in range(steps):
        part = pl.ds(i * chunk, chunk)
        loads.append(pltpu.make_async_copy(wave_ref.at[:, part, :], wf.at[i % 2], wave_sem.at[i]))
    load_local = pltpu.make_async_copy(wave_ref.at[:, :, lanes], wloc, local.at[1])
    load_left = pltpu.make_async_copy(left_ref, lefts.at[0], local.at[2])

    others = [lax.rem(band + i, 4) for i in range(1, 4)]
    places = [(ring.peer(i), band) for i in range(1, slots)] + [(me, other) for other in others]
    barrier = pltpu.get_barrier_semaphore()
    for place in places:
        pl.semaphore_signal(barrier, inc=1, device_id=place, device_id_type=pl.DeviceIdType.MESH)

    def first(i):
        other = lax.rem(i, 2)
        source = pack.at[i // 2, ring.y + other * (1 - 2 * ring.y), band]
        return remote(source, ops.at[i, band], first_s.at[i - 1], first_l.at[i - 1], (ring.peer(i), band))

    def far(i):
        block = ops.at[i, band]
        return remote(block, block, far_s.at[i - 1], far_l.at[i - 1], (me, ring.far))

    def near(i):
        block = ops.at[i, band]
        return remote(block, block, near_s.at[i - 1], near_l.at[i - 1], (me, ring.near))

    def last(i):
        block = ops.at[i, ring.far]
        return remote(block, block, last_s.at[i - 1], last_l.at[i - 1], (me, ring.near))

    def tile(i):
        return remote(tiles.at[0], tiles.at[i], tile_s.at[i - 1], tile_l.at[i - 1], (ring.peer(i), band))

    def over(j):
        source, step = (lefts.at[4], 1) if j == 3 else (left_ref, j)
        return remote(source, lefts.at[2 * j], left_s.at[j - 1], left_l.at[j - 1], (ring.peer(2 * step), band))

    def twin(j):
        source = lefts.at[2 * j] if j else left_ref
        return remote(source, lefts.at[2 * j + 1], twin_s.at[j], twin_l.at[j], (ring.peer(1), band))

    load_right.wait()
    load_local.start()
    for load in loads[:2]:
        load.start()
    load_left.start()
    keep = pltpu.make_async_copy(pack.at[0, ring.y], ops.at[0], local.at[4])
    for j in range(slots // 2):
        pack_pair(rv, pack, j, ring.zs[j])
        if j == 0:
            keep.start()
            pl.semaphore_wait(barrier, len(places))
            first(1).start()
        elif j < 3:
            first(2 * j).start()
            first(2 * j + 1).start()
    load_site.wait()
    tiles[0] = jnp.concatenate([site[...]] * (LANES // phys), axis=1)
    for i in range(1, slots):
        tile(i).start()

    def forward(i):
        first(i).wait_recv()
        far(i).start()
        near(i).start()

    load_local.wait()
    local_weights(wloc, gh, gl, ring.y, phys, 0, phys // 2)
    for i in range(1, 4):
        forward(i)
    first(6).start()
    first(7).start()
    twin(0).start()
    over(1).start()
    for i in range(steps):
        loads[i].wait()
        split_rows(wf, wh, wl, i % 2, i * chunk)
        if i + 2 < steps:
            loads[i + 2].start()
    for i in range(1, 4):
        far(i).wait_recv()
        last(i).start()
    local_weights(wloc, gh, gl, ring.y, phys, phys // 2, phys)
    for i in range(1, slots):
        tile(i).wait_recv()
    site_blocks(tiles, dd)
    keep.wait()
    for i in range(1, 4):
        near(i).wait_recv()
        last(i).wait_recv()
    right_planes(ops, rh, rl, 0)

    height = flat // 4

    def make(step, xs):
        act_rows(wh, wl, rh, rl, xs, step, height)

    def use(step, xs):
        site_rows(dd, xs, yh, yl, step, phys)

    order = (2, 3, 1, 0)

    def fold_one(j, half):
        sem = 4 * half + j
        place = (ring.peer(2 if j == 1 else 1), band)
        return remote(nb.at[2 * j + 1, half], n1.at[j, half], n1_s.at[sem], n1_l.at[sem], place)

    def fold_two(j, half):
        sem = 3 * half + j - 1
        return remote(nb.at[2 * j, half], n2.at[j - 1, half], n2_s.at[sem], n2_l.at[sem], (ring.peer(2 * j), band))

    def news(half):
        part = rows // 2
        overlaps(yh, yl, gh, gl, qs, range(4, 8), slice(half * part, (half + 1) * part))
        for j in (1, 2, 3, 0):
            new_part(source_ref, coupling_ref, owner_ref, qs, nb, 2 * j + 1, half, ring, rows)
            if j:
                fold_one(j, half).start()
        for j in order:
            new_part(source_ref, coupling_ref, owner_ref, qs, nb, 2 * j, half, ring, rows)
            if j == 1:
                fold_two(j, half).start()

    def gather_news(j, half):
        fold_one(j, half).wait_recv()
        spot = 1 if j == 1 else 2 * j
        nb[spot, half] += n1[j, half]
        if j == 1:
            fold_one(0, half).start()
        elif j:
            fold_two(j, half).start()

    forward(4)
    forward(5)

    def act_two(u, carry):
        @pl.when(u == 1)
        def _():
            forward(6)
            forward(7)
            for i in range(4, 6):
                far(i).wait_recv()
                last(i).start()
            over(2).start()
            over(1).wait_recv()
            twin(1).start()

        @pl.when(u == 2)
        def _():
            for i in range(6, 8):
                far(i).wait_recv()
                last(i).start()
            overlaps(yh, yl, gh, gl, qs, range(4), slice(0, rows))
            for i in range(4, 8):
                near(i).wait_recv()
                last(i).wait_recv()
            right_planes(ops, rh, rl, 1)
            over(2).wait_recv()
            over(3).start()
            twin(2).start()

        @pl.when(u == 3)
        def _():
            over(3).wait_recv()
            twin(3).start()
            news(0)

        make(2 * u, xa)
        make(2 * u + 1, xb)
        use(2 * u, xa)
        use(2 * u + 1, xb)
        return carry

    for small in smalls:
        small.wait()
    lax.fori_loop(0, 4, act_two, 0)
    gather_news(1, 0)
    gather_news(2, 0)
    news(1)
    gather_news(3, 0)
    load_left.wait()
    for j in range(4):
        twin(j).wait_recv()
    entries, flags = by_charge(charge_ref, ring, slots)
    left_stack(lefts, lh, ll, entries)

    above = lax.rem(band + 1, 4)

    def lift(pair):
        part = pl.ds(2 * pair, 2)
        return remote(up.at[:, part], moved.at[:, part], up_s.at[pair], up_l.at[pair], (me, above))

    def close_step(step, carry):
        @pl.when(step == 1)
        def _():
            gather_news(0, 0)
            gather_news(1, 1)
            gather_news(2, 1)

        @pl.when(step == 2)
        def _():
            gather_news(3, 1)

        @pl.when(step == 3)
        def _():
            gather_news(0, 1)

        for pair in (2 * step, 2 * step + 1):
            close_pair(lh, ll, yh, yl, sigma_ref, up, pair, entries, flags)

        @pl.when(band < 3)
        def _():
            lift(2 * step).start()
            lift(2 * step + 1).start()

        return carry

    lax.fori_loop(0, phys // 4, close_step, 0)

    def store(pair):
        part = pl.ds(2 * pair, 2)
        return pltpu.make_async_copy(sigma_ref.at[:, part], sigma_hbm.at[:, part], out_sem.at[pair])

    def gain(pair, carry):
        @pl.when(band > 0)
        def _():
            lift(pair).wait_recv()
            part = pl.ds(2 * pair, 2)
            sigma_ref[:, part] += moved[:, part]

        store(pair).start()
        return carry

    lax.fori_loop(0, phys // 2, gain, 0)
    for half in range(2):
        for j in order[:3]:
            fold_two(j, half).wait_recv()
        for part in range(2):
            total = nb[0, half, part]
            for j in order[:3]:
                total = total + n2[j - 1, half, part]
            start = part * rows + half * (rows // 2)
            new_ref[start : start + rows // 2, :] = total
    store_new = pltpu.make_async_copy(new_ref, new_hbm, out_sem.at[phys // 2])
    store_new.start()

    for i in range(1, slots):
        for copy in (first(i), far(i), near(i), last(i), tile(i)):
            copy.wait_send()
    for j in range(4):
        twin(j).wait_send()
        if j:
            over(j).wait_send()
        for half in range(2):
            fold_one(j, half).wait_send()
            if j:
                fold_two(j, half).wait_send()

    @pl.when(band < 3)
    def _():
        for pair in range(phys // 2):
            lift(pair).wait_send()

    store_new.wait()
    for pair in range(phys // 2):
        store(pair).wait()


def whole(charge, source, coupling, owner, wave, right, left, site):
    _, flat, bond = wave.shape
    terms = charge.shape[0]
    phys = site.shape[1]
    cols = bond // terms
    rows = flat // phys
    lines = terms * rows
    f32, bf16 = jnp.float32, jnp.bfloat16
    hbm = pl.BlockSpec(memory_space=pl.ANY)
    dma = lambda n: pltpu.SemaphoreType.DMA((n,))
    return pl.pallas_call(
        whole_kernel,
        in_specs=[hbm] * 8,
        out_specs=[hbm] * 2,
        out_shape=[
            jax.ShapeDtypeStruct((2, phys, cols, rows), f32),
            jax.ShapeDtypeStruct((2 * rows, rows), f32),
        ],
        scratch_shapes=[
            pltpu.SMEM(charge.shape, jnp.int32),
            pltpu.SMEM(source.shape, jnp.int32),
            pltpu.SMEM(coupling.shape, f32),
            pltpu.SMEM(owner.shape, jnp.int32),
            pltpu.VMEM(site.shape, f32),
            pltpu.VMEM((2, 2, flat // 4, bond), f32),
            pltpu.VMEM((2, flat, LANES), f32),
            pltpu.VMEM((3, flat, bond), bf16),
            pltpu.VMEM((3, flat, bond), bf16),
            pltpu.VMEM(right.shape, f32),
            pltpu.VMEM((terms // 2, 2, 4, bond // 4, LANES), f32),
            pltpu.VMEM((terms, 4, bond // 4, LANES), f32),
            pltpu.VMEM((terms, 2 * phys, LANES), f32),
            pltpu.VMEM((terms,) + left.shape, f32),
            pltpu.VMEM((2, phys, cols, rows), f32),
            pltpu.VMEM((2 * rows, rows), f32),
            pltpu.VMEM((2, 3, bond, 2 * LANES), bf16),
            pltpu.VMEM((2, 3, bond, 2 * LANES), bf16),
            pltpu.VMEM((terms, 16 * phys, 16 * phys), bf16),
            pltpu.VMEM((flat, 2 * rows), bf16),
            pltpu.VMEM((flat, 2 * rows), bf16),
            pltpu.VMEM((4, 2, 2, flat // 4, LANES), bf16),
            pltpu.VMEM((4, 2, 2, flat // 4, LANES), bf16),
            pltpu.VMEM((phys, terms, rows, LANES), bf16),
            pltpu.VMEM((phys, terms, rows, LANES), bf16),
            pltpu.VMEM((lines, 2 * LANES), f32),
            pltpu.VMEM((2 * rows, lines + 2 * rows), bf16),
            pltpu.VMEM((2 * rows, lines + 2 * rows), bf16),
            pltpu.VMEM((terms, 2, 2, rows // 2, rows), f32),
            pltpu.VMEM((terms // 2, 2, 2, rows // 2, rows), f32),
            pltpu.VMEM((terms // 2 - 1, 2, 2, rows // 2, rows), f32),
            pltpu.VMEM((2, phys, cols, rows), f32),
            pltpu.VMEM((2, phys, cols, rows), f32),
            dma(phys // 2 + 1),
            dma(5),
            dma(4),
            dma(4),
        ]
        + [dma(terms - 1)] * 10
        + [dma(terms // 2 - 1)] * 2
        + [dma(terms // 2)] * 2
        + [dma(terms)] * 2
        + [dma(terms - 2)] * 2
        + [dma(phys // 2)] * 2,
        compiler_params=pltpu.CompilerParams(
            collective_id=2, has_side_effects=True, vmem_limit_bytes=56 * 1024 * 1024
        ),
    )(charge, source, coupling, owner, wave, right, left, site)


def hand_kernel(sigma_ref, new_ref, sigma_out, new_out, sigma_mid, new_mid, ins, outs):
    parts = outs.shape[0] - 1
    width = sigma_ref.shape[1] // parts
    places = [(new_ref, new_mid, new_out)]
    for i in range(parts):
        part = pl.ds(i * width, width)
        places.append((sigma_ref.at[:, part], sigma_mid.at[:, part], sigma_out.at[:, part]))
    loads = [pltpu.make_async_copy(a, b, ins.at[i]) for i, (a, b, _) in enumerate(places)]
    stores = [pltpu.make_async_copy(b, c, outs.at[i]) for i, (_, b, c) in enumerate(places)]
    for load in loads:
        load.start()
    for load, store in zip(loads, stores):
        load.wait()
        store.start()
    for store in stores:
        store.wait()


def hand(sigma, new):
    spec = [pl.BlockSpec(memory_space=pl.ANY)] * 2
    return pl.pallas_call(
        hand_kernel,
        in_specs=spec,
        out_specs=spec,
        out_shape=[jax.ShapeDtypeStruct(v.shape, v.dtype) for v in (sigma, new)],
        scratch_shapes=[pltpu.VMEM(v.shape, v.dtype) for v in (sigma, new)] + [pltpu.SemaphoreType.DMA((5,))] * 2,
        compiler_params=pltpu.CompilerParams(vmem_limit_bytes=60 * 1024 * 1024),
    )(sigma, new)


def block(wave, left, right, site, charge, source, coupling, owner):
    _, rows, phys, bond = wave.shape
    sigma, new = whole(
        charge,
        source.T,
        coupling.transpose(2, 0, 1),
        owner,
        wave.reshape(2, rows * phys, bond),
        right[0],
        left[0].reshape(2 * rows, rows),
        site[0].reshape(2 * phys, phys),
    )
    sigma, new = hand(sigma, new)
    return sigma.transpose(0, 3, 1, 2), new.reshape(1, 2, rows, rows)


def body(wave, left, right, site, charge, source, coupling, owner):
    _, rows, phys, bond = wave.shape
    terms = lax.axis_size("terms")
    bands = lax.axis_size("sect")
    me = lax.axis_index("terms")
    cols = bond // terms
    per = LANES // cols
    pack = packed(right[0], terms).reshape(terms, bands, -1, LANES)
    lines = site.size // LANES
    room = -lines % 8
    small = jnp.concatenate(
        (left[0].reshape(2 * rows, rows), site.reshape(lines, LANES), jnp.zeros((room, LANES), jnp.float32))
    )
    ops, smalls = gather(pack, small)
    sites = smalls[:, 2 * rows : 2 * rows + lines].reshape(terms // per, per, 2, phys, phys)
    weights = jnp.stack((sites[:, :, 0], sites[:, :, 1], sites[:, :, 0] + sites[:, :, 1]))
    slot = jnp.arange(LANES, dtype=jnp.int32) // cols
    coef = sum(jnp.where(slot == j, weights[:, :, j, :, :, None], 0.0) for j in range(per))
    y = act(wave.reshape(2, rows * phys, bond), ops.reshape(terms, 2, bond // per, LANES), coef, phys)
    local = lax.dynamic_slice_in_dim(wave, me * cols, cols, axis=3).reshape(2 * rows, phys * cols)
    term_ids = jnp.arange(terms, dtype=jnp.int32)
    hit = (source[:, :, None] == term_ids).astype(jnp.float32)
    place = (owner[None, :] == term_ids[:, None]).astype(jnp.float32)
    weight = jnp.sum(coupling[:, :, :, None] * hit, axis=2)
    weight = jnp.sum(place[None, :, :, None] * weight[:, None], axis=2)
    stay, up, part = close(charge, weight, y, smalls, local)
    sigma, new = finish(stay, up, part)
    return sigma.reshape(2, rows, phys, cols), new.reshape(1, 2, rows, rows)


def solution(mesh):
    placed = (
        P(None, "sect", None, None),
        P("terms", None, "sect", None),
        P("terms", None, None, None),
        P("terms", None, None, None),
        P(),
        P(),
        P(),
        P(),
    )
    fits = mesh.shape["terms"] == 8 and mesh.shape["sect"] == 4
    return jax.shard_map(
        block if fits else body,
        mesh=mesh,
        in_specs=placed,
        out_specs=(P(None, "sect", None, "terms"), P("terms", None, "sect", None)),
        check_vma=False,
    )
```
